128 devices in a mesh: dp: 4 (over y_lo, core), ctx: 32 (over z, x, y_hi).
Axes of the slice: x: 4, y: 4 (y_hi: 2, y_lo: 2; y = y_hi * 2 + y_lo), z: 4, core: 2. Of those that a mesh axis runs over, the one named last changes fastest.
Arguments:
- queries: bfloat16 [4, 32768, 1024], P('dp', 'ctx'), may hold values from -160 to 160
- keys: bfloat16 [4, 32768, 1024], P('dp', 'ctx'), may hold values from -14 to 14
- values: bfloat16 [4, 32768, 1024], P('dp', 'ctx'), may hold values from -4.5 to 4.5
- cotangent: bfloat16 [4, 32768, 1024], P('dp', 'ctx'), may hold values from -6 to 6
- gain: float32 [1024], replicated, may hold values from 0.1 to 1.9
Outputs:
- attended: bfloat16 [4, 32768, 1024], P('dp', 'ctx')
- grad_queries: bfloat16 [4, 32768, 1024], P('dp', 'ctx')
- grad_keys: bfloat16 [4, 32768, 1024], P('dp', 'ctx')
- grad_values: bfloat16 [4, 32768, 1024], P('dp', 'ctx')
- gain_grad: float32 [1024], replicated
The draws below stay inside these ranges and needn't reach their ends.
All inputs are finite; a program needn't handle non-finite values.
Results may differ from the reference program's by a relative error of at most 0.019.
The reference program's roundings to bfloat16 on the way count: a program that leaves them out, or rounds other values in their place, can miss the bound.
Values may be sent and summed in bfloat16 or wider, within the bound.
A program may use at most 192 MiB of HBM per device.

```python
import jax
import jax.numpy as jnp
from jax import lax

H = 8
HD = 128
BLOCK = 128
STRIDE = 1024
SUMMARY = 8
D = 1024
SEQ = 32768
BATCH = 4


def shared_keys(key):
    base = jnp.clip(jax.random.normal(jax.random.fold_in(key, 11), (BATCH, SEQ, H * HD), jnp.float32), -4.5, 4.5)
    return base


def draw_keys(key, part):
    return shared_keys(key).astype(jnp.bfloat16)


def draw_queries(key, part):
    noise = jnp.clip(jax.random.normal(jax.random.fold_in(key, 13), (BATCH, SEQ, H * HD), jnp.float32), -4.5, 4.5) * 2.0
    return noise.astype(jnp.bfloat16)


def levels(stream_key, shape, shards, smallest, top_value):
    factor_of = 1.0
    for dim, parts in shards:
        steps = jax.random.uniform(jax.random.fold_in(jax.random.fold_in(stream_key, 6), dim), (parts,), jnp.float32, smallest / len(shards), top_value / len(shards))
        factor_of = factor_of * jnp.repeat(jnp.exp(steps), shape[dim] // parts).reshape((-1,) + (1,) * (len(shape) - 1 - dim))
    return factor_of


def gaussian(own_key, shape, deviation, most, split=(), held_as=jnp.bfloat16):
    factor_of = levels(own_key, shape, split, -0.22, 0.18) if split else 1.0
    drawn = jax.random.normal(own_key, shape, jnp.float32) * deviation * factor_of
    return jnp.minimum(jnp.maximum(drawn, -most), most).astype(held_as)


def setup_inputs(seed: int = 0) -> dict:
    key_list = jax.random.split(jax.random.key(seed), 6)
    queries = draw_queries(jax.random.fold_in(key_list[5], 71), 0)
    keys = draw_keys(jax.random.fold_in(key_list[5], 71), 0)
    values = gaussian(key_list[2], (BATCH, SEQ, D), 1.0, 4.5, ((0, 4), (1, 32)))
    cotangent = gaussian(key_list[3], (BATCH, SEQ, D), 1.0, 6.0, ((0, 4), (1, 32)))
    gain = jnp.clip(1.0 + 0.18 * jax.random.normal(key_list[4], (D,), jnp.float32), 0.1, 1.9)
    return {"queries": queries, "keys": keys, "values": values, "cotangent": cotangent, "gain": gain}


NEG = -1e30


def to_rows(block_array):
    blocks, heads, width = block_array.shape
    return block_array.transpose(1, 0, 2).reshape(heads, blocks * width)


def to_blocks(row_array, blocks):
    heads, length = row_array.shape
    return row_array.reshape(heads, blocks, length // blocks).transpose(1, 0, 2)


def sequence_pass(queries, keys, values, cotangent, gain):
    f32 = jnp.float32
    bf16 = jnp.bfloat16
    length = queries.shape[0]
    blocks = length // BLOCK
    segs = length // STRIDE
    total_sums = segs * SUMMARY
    scale = HD ** -0.5
    scaled = (queries.astype(f32) * gain).astype(bf16)
    padding = jnp.zeros((BLOCK, H * HD), bf16)
    ext_keys = jnp.concatenate([padding, keys], 0).reshape(blocks + 1, BLOCK, H, HD)
    ext_values = jnp.concatenate([padding, values], 0).reshape(blocks + 1, BLOCK, H, HD)
    band_keys = jnp.concatenate([ext_keys[:-1], ext_keys[1:]], 1)
    band_values = jnp.concatenate([ext_values[:-1], ext_values[1:]], 1)
    query_blocks = scaled.reshape(blocks, BLOCK, H, HD)
    scaled_rows = scaled.reshape(length, H, HD)
    sum_keys = keys.reshape(segs, STRIDE, H * HD)[:, STRIDE - SUMMARY:].reshape(total_sums, H, HD)
    sum_values = values.reshape(segs, STRIDE, H * HD)[:, STRIDE - SUMMARY:].reshape(total_sums, H, HD)
    query_index = jnp.arange(BLOCK)[:, None]
    key_index = jnp.arange(2 * BLOCK)[None, :]
    band = (key_index > query_index) & (key_index <= query_index + BLOCK)
    later_block = jnp.arange(blocks)[:, None, None] > 0
    band_mask = (band[None] & (later_block | (key_index >= BLOCK)[None]))[:, None]
    slot = jnp.arange(total_sums)
    sum_pos = (slot // SUMMARY) * STRIDE + STRIDE - SUMMARY + slot % SUMMARY
    query_pos = jnp.arange(length)
    sum_mask = (query_pos[:, None] - sum_pos[None, :] >= BLOCK)[None]
    band_scores = jnp.einsum("nqhd,nkhd->nhqk", query_blocks.astype(f32), band_keys.astype(f32)) * scale
    band_scores = jnp.where(band_mask, band_scores, NEG)
    sum_scores = jnp.einsum("qhd,shd->hqs", scaled_rows.astype(f32), sum_keys.astype(f32)) * scale
    sum_scores = jnp.where(sum_mask, sum_scores, NEG)
    top = jnp.maximum(to_rows(jnp.max(band_scores, -1)), jnp.max(sum_scores, -1))
    band_exp = jnp.where(band_mask, jnp.exp(band_scores - to_blocks(top, blocks)[..., None]), 0.0)
    sum_exp = jnp.where(sum_mask, jnp.exp(sum_scores - top[..., None]), 0.0)
    total = to_rows(jnp.sum(band_exp, -1)) + jnp.sum(sum_exp, -1)
    band_prob = band_exp / to_blocks(total, blocks)[..., None]
    sum_prob = sum_exp / total[..., None]
    band_prob_b = band_prob.astype(bf16)
    sum_prob_b = sum_prob.astype(bf16)
    mixed = jnp.einsum("nhqk,nkhd->nqhd", band_prob_b.astype(f32), band_values.astype(f32)).reshape(length, H, HD)
    mixed = mixed + jnp.einsum("hqs,shd->qhd", sum_prob_b.astype(f32), sum_values.astype(f32))
    attended = mixed.reshape(length, H * HD).astype(bf16)
    grad_rows = cotangent.reshape(length, H, HD).astype(f32)
    grad_blocks = grad_rows.reshape(blocks, BLOCK, H, HD)
    delta = jnp.sum(grad_rows * attended.reshape(length, H, HD).astype(f32), -1).T
    band_dprob = jnp.einsum("nqhd,nkhd->nhqk", grad_blocks, band_values.astype(f32))
    sum_dprob = jnp.einsum("qhd,shd->hqs", grad_rows, sum_values.astype(f32))
    band_ds = (band_prob * (band_dprob - to_blocks(delta, blocks)[..., None]) * scale).astype(bf16)
    sum_ds = (sum_prob * (sum_dprob - delta[..., None]) * scale).astype(bf16)
    band_dv = jnp.einsum("nhqk,nqhd->nkhd", band_prob_b.astype(f32), grad_blocks)
    band_dk = jnp.einsum("nhqk,nqhd->nkhd", band_ds.astype(f32), query_blocks.astype(f32))

    def fold_band(pairs):
        later = jnp.concatenate([pairs[1:, :BLOCK], jnp.zeros((1, BLOCK, H, HD), f32)], 0)
        return (pairs[:, BLOCK:] + later).reshape(segs, STRIDE, H * HD)

    sum_dv = jnp.einsum("hqs,qhd->shd", sum_prob_b.astype(f32), grad_rows).reshape(segs, SUMMARY, H * HD)
    sum_dk = jnp.einsum("hqs,qhd->shd", sum_ds.astype(f32), scaled_rows.astype(f32)).reshape(segs, SUMMARY, H * HD)
    grad_values = fold_band(band_dv).at[:, STRIDE - SUMMARY:].add(sum_dv).reshape(length, H * HD).astype(bf16)
    grad_keys = fold_band(band_dk).at[:, STRIDE - SUMMARY:].add(sum_dk).reshape(length, H * HD).astype(bf16)
    grad_scaled = jnp.einsum("nhqk,nkhd->nqhd", band_ds.astype(f32), band_keys.astype(f32)).reshape(length, H, HD)
    grad_scaled = grad_scaled + jnp.einsum("hqs,shd->qhd", sum_ds.astype(f32), sum_keys.astype(f32))
    grad_scaled = grad_scaled.reshape(length, H * HD)
    grad_queries = (grad_scaled * gain).astype(bf16)
    gain_part = jnp.sum(grad_scaled * queries.astype(f32), 0)
    return attended, grad_queries, grad_keys, grad_values, gain_part


def reference(queries, keys, values, cotangent, gain):
    results = lax.map(lambda items: sequence_pass(items[0], items[1], items[2], items[3], gain), (queries, keys, values, cotangent))
    attended, grad_queries, grad_keys, grad_values, gain_parts = results
    gain_grad = jnp.sum(gain_parts, 0) * (BATCH * SEQ) ** -0.5
    return attended, grad_queries, grad_keys, grad_values, gain_grad
```

```python
import functools

import jax
import jax.numpy as jnp
from jax import lax
from jax.experimental import pallas as pl
from jax.experimental.pallas import tpu as pltpu
from jax.sharding import PartitionSpec as P

f32 = jnp.float32
bf16 = jnp.bfloat16
MESH = pl.DeviceIdType.MESH

H = 8
HD = 128
BLOCK = 128
STRIDE = 1024
SUMMARY = 8
SCALE = HD**-0.5
LOG2E = 1.4426950408889634
NEG = -1e30
TILE = 256
PARTS = 2


def nt(a, b):
    return lax.dot_general(a, b, (((1,), (1,)), ((), ())), preferred_element_type=f32)


def nn(a, b):
    return lax.dot_general(a, b, (((1,), (0,)), ((), ())), preferred_element_type=f32)


def attend_head(rank, q_ref, do_ref, kx, vx, sk, sv, gain, o_ref, gq_ref, gk_ref, gv_ref):
    length = q_ref.shape[0]
    blocks = length // BLOCK
    nb = TILE // BLOCK
    slots = sk.shape[0]
    skT, svT, kxT, vxT = sk.T, sv.T, kx.T, vx.T
    before = lax.broadcasted_iota(jnp.int32, (BLOCK, BLOCK), 0) > lax.broadcasted_iota(
        jnp.int32, (BLOCK, BLOCK), 1
    )
    dk, dv = [None] * (blocks + 1), [None] * (blocks + 1)
    dsk = dsv = gp = None
    plus = lambda old, new: new if old is None else old + new
    none = jnp.zeros((BLOCK, BLOCK), bf16)

    for t in range(length // TILE):
        rows = pl.ds(t * TILE, TILE)
        first = t * nb
        near = slice(first * BLOCK, (first + nb + 1) * BLOCK)
        qf = q_ref[rows, :].astype(f32)
        qs = (qf * gain).astype(bf16)
        do = do_ref[rows, :]

        def band(full, start):
            columns = []
            for i in range(nb):
                lanes = slice(i * BLOCK, (i + 1) * BLOCK)
                earlier = full[i * BLOCK : (i + 1) * BLOCK, lanes]
                if start is not None and t == 0 and i == 0:
                    earlier = jnp.where(rank > 0, earlier, start)
                columns.append(jnp.where(before, earlier, full[(i + 1) * BLOCK : (i + 2) * BLOCK, lanes]))
            return jnp.concatenate(columns, 1)

        sb = band(nt(kx[near], qs), NEG)
        db = band(nt(vx[near], do), None)
        ss = nt(sk, qs)
        ds = nt(sv, do)
        slot = lax.broadcasted_iota(jnp.int32, (slots, TILE), 0)
        if t == 0:
            spos = slot // SUMMARY * STRIDE + STRIDE - SUMMARY + slot % SUMMARY
            qpos = rank * length + lax.broadcasted_iota(jnp.int32, (slots, TILE), 1)
            seen = qpos - spos >= BLOCK
        else:
            seen = slot < SUMMARY * rank
        ss = jnp.where(seen, ss, NEG)
        top = jnp.maximum(jnp.max(sb, 0, keepdims=True), jnp.max(ss, 0, keepdims=True))
        eb = jnp.exp2((sb - top) * (SCALE * LOG2E))
        es = jnp.exp2((ss - top) * (SCALE * LOG2E))
        inv = 1.0 / (jnp.sum(eb, 0, keepdims=True) + jnp.sum(es, 0, keepdims=True))
        pb, ps = eb * inv, es * inv
        delta = jnp.sum(pb * db, 0, keepdims=True) + jnp.sum(ps * ds, 0, keepdims=True)
        gb = pb * ((db - delta) * SCALE)
        gs = ps * ((ds - delta) * SCALE)

        def unfold(x, xs):
            strips = []
            for j in range(nb + 1):
                cells = []
                for i in range(nb):
                    cell = x[:, i * BLOCK : (i + 1) * BLOCK]
                    if j == i:
                        cells.append(jnp.where(before, cell, 0.0).astype(bf16))
                    elif j == i + 1:
                        cells.append(jnp.where(before, 0.0, cell).astype(bf16))
                    else:
                        cells.append(none)
                strips.append(jnp.concatenate(cells, 1))
            return jnp.concatenate(strips + [xs.astype(bf16)], 0)

        prob, dscore = unfold(pb, ps), unfold(gb, gs)
        dvt, dkt = nn(prob, do), nn(dscore, qs)
        for j in range(nb + 1):
            strip = slice(j * BLOCK, (j + 1) * BLOCK)
            dv[first + j] = plus(dv[first + j], dvt[strip])
            dk[first + j] = plus(dk[first + j], dkt[strip])
        dsv = plus(dsv, dvt[(nb + 1) * BLOCK :])
        dsk = plus(dsk, dkt[(nb + 1) * BLOCK :])
        o_ref[rows, :] = nn(jnp.concatenate([vxT[:, near], svT], 1), prob).T.astype(bf16)
        dq = nn(jnp.concatenate([kxT[:, near], skT], 1), dscore).T
        gq_ref[rows, :] = (dq * gain).astype(bf16)
        gp = plus(gp, jnp.sum(dq * qf, 0, keepdims=True))
        for j in range(nb):
            n = first + j
            if n > 0:
                gk_ref[pl.ds((n - 1) * BLOCK, BLOCK), :] = dk[n].astype(bf16)
                gv_ref[pl.ds((n - 1) * BLOCK, BLOCK), :] = dv[n].astype(bf16)
    return dk[0], dv[0], dk[blocks], dv[blocks], dsk, dsv, gp


def exchange_kernel(
    q_ref, do_ref, k_ref, v_ref, g_ref, k_all, v_all,
    o_ref, gq_ref, gk_out, gv_out, gain_out,
    rim, mine, sums, grim, rrim, gsum, rsum, gk, gv, tail, acc, gbuf, gsub, gall,
    rim_s, rim_r, sum_s, sum_r, grim_s, grim_r, gsum_s, gsum_r, ga_s, ga_r, gb_s, gb_r, loc, put,
):
    h = pl.program_id(0)
    dp, rank = lax.axis_index("dp"), lax.axis_index("ctx")
    dps, ranks = lax.axis_size("dp"), lax.axis_size("ctx")
    length = q_ref.shape[0]
    half = H // PARTS
    last = length - BLOCK
    pair, side = rank // 2, rank % 2
    cell, cells = dp * 2 + side, dps * 2
    pairs = ranks // 2

    def rim_copy(i, which):
        src = (k_all, v_all)[which].at[pl.ds(last, BLOCK), pl.ds(i * HD, HD)]
        return pltpu.make_async_remote_copy(
            src, rim.at[i, which], rim_s.at[i, which], rim_r.at[i, which],
            device_id={"ctx": jnp.minimum(rank + 1, ranks - 1)}, device_id_type=MESH,
        )

    def sum_copy(source, target):
        return pltpu.make_async_remote_copy(
            mine, sums.at[source], sum_s.at[target], sum_r.at[source],
            device_id={"ctx": target}, device_id_type=MESH,
        )

    def grim_copy(i):
        return pltpu.make_async_remote_copy(
            grim.at[i], rrim.at[i], grim_s.at[i], grim_r.at[i],
            device_id={"ctx": jnp.maximum(rank - 1, 0)}, device_id_type=MESH,
        )

    def gsum_copy(part, source, target):
        return pltpu.make_async_remote_copy(
            gsum.at[part, target], rsum.at[part, source], gsum_s.at[part, target], gsum_r.at[part, source],
            device_id={"ctx": target}, device_id_type=MESH,
        )

    def cell_copy(source, target):
        return pltpu.make_async_remote_copy(
            gbuf, gsub.at[source], ga_s.at[target], ga_r.at[source],
            device_id={"dp": target // 2, "ctx": pair * 2 + target % 2}, device_id_type=MESH,
        )

    def pair_copy(source, target):
        return pltpu.make_async_remote_copy(
            gsub.at[cell], gall.at[source], gb_s.at[target], gb_r.at[source],
            device_id={"ctx": target * 2 + side}, device_id_type=MESH,
        )

    def put_copy(i, which):
        lanes = pl.ds(pl.multiple_of(i * HD, HD), HD)
        out, held = ((gk_out, gk), (gv_out, gv))[which]
        return pltpu.make_async_copy(
            held.at[i % 2], out.at[pl.ds(0, last), lanes], put.at[i % 2, which]
        )

    def each(count, body, start=0):
        lax.fori_loop(start, count, lambda i, c: (body(i), c)[1], 0)

    @pl.when(h == 0)
    def _():
        own = [
            pltpu.make_async_copy(full.at[pl.ds(length - SUMMARY, SUMMARY), :], mine.at[i], loc.at[i])
            for i, full in enumerate((k_all, v_all))
        ]
        for copy in own:
            copy.start()
        barrier = pltpu.get_barrier_semaphore()

        def greet_rank(t):
            @pl.when(t != rank)
            def _():
                pl.semaphore_signal(barrier, inc=1, device_id={"ctx": t}, device_id_type=MESH)

        def greet_cell(c):
            @pl.when(c // 2 != dp)
            def _():
                pl.semaphore_signal(
                    barrier, inc=1, device_id={"dp": c // 2, "ctx": pair * 2 + c % 2}, device_id_type=MESH
                )

        each(ranks, greet_rank)
        each(cells, greet_cell)
        pl.semaphore_wait(barrier, ranks - 1 + cells - 2)

        @pl.when(rank < ranks - 1)
        def _():
            for which in range(2):
                rim_copy(0, which).start()

        for copy in own:
            copy.wait()
        each(ranks, lambda t: sum_copy(rank, t).start(), rank + 1)

        @pl.when(rank < ranks - 1)
        def _():
            for i in range(1, H):
                for which in range(2):
                    rim_copy(i, which).start()

        each(rank, lambda s: sum_copy(s, rank).wait_recv())

    @pl.when(rank > 0)
    def _():
        for which in range(2):
            rim_copy(h, which).wait_recv()

    @pl.when(h >= 2)
    def _():
        for which in range(2):
            put_copy(h - 2, which).wait()

    lanes = pl.ds(pl.multiple_of(h * HD, HD), HD)
    slots = sums.shape[0] * SUMMARY
    there = lax.broadcasted_iota(jnp.int32, (slots, HD), 0) < SUMMARY * rank

    def summary(which):
        rows = sums[:, which, :, lanes].astype(f32).reshape(slots, HD)
        return jnp.where(there, rows, 0.0).astype(bf16)

    def extended(which, ref):
        edge = jnp.where(rank > 0, rim[h, which], jnp.zeros((BLOCK, HD), bf16))
        return jnp.concatenate([edge, ref[...]], 0)

    dk0, dv0, dkn, dvn, dsk, dsv, gp = attend_head(
        rank, q_ref, do_ref, extended(0, k_ref), extended(1, v_ref), summary(0), summary(1), g_ref[...],
        o_ref, gq_ref, gk.at[h % 2], gv.at[h % 2],
    )
    for which in range(2):
        put_copy(h, which).start()
    grim[h, 0] = dk0.astype(bf16)
    grim[h, 1] = dv0.astype(bf16)
    tail[h, 0] = dkn
    tail[h, 1] = dvn
    part = h // half
    inner = pl.ds(pl.multiple_of(h % half * HD, HD), HD)
    gsum[part, :, 0, :, inner] = dsk.reshape(slots // SUMMARY, SUMMARY, HD).astype(bf16)
    gsum[part, :, 1, :, inner] = dsv.reshape(slots // SUMMARY, SUMMARY, HD).astype(bf16)
    gbuf[pl.ds(h, 1), :] = gp

    @pl.when(rank > 0)
    def _():
        grim_copy(h).start()

    @pl.when(h % half == half - 1)
    def _():
        each(rank, lambda t: gsum_copy(part, rank, t).start())

    @pl.when(h == H - 1)
    def _():
        def others(count, me, body):
            def one(i):
                @pl.when(i != me)
                def _():
                    body(i)

            each(count, one)

        others(cells, cell, lambda c: cell_copy(cell, c).start())
        others(cells, cell, lambda c: cell_copy(c, cell).wait_recv())
        others(cells, cell, lambda c: cell_copy(cell, c).wait_send())
        gsub[cell] = gbuf[...]
        total = gsub[0]
        for c in range(1, gsub.shape[0]):
            total = total + gsub[c]
        gsub[cell] = total
        gall[pair] = total
        others(pairs, pair, lambda p: pair_copy(pair, p).start())

        for p in range(PARTS):
            acc[p] = jnp.zeros(acc.shape[1:], f32)

        def collect(s):
            for p in range(PARTS):
                gsum_copy(p, s, rank).wait_recv()
                acc[p] = acc[p] + rsum[p, s].astype(f32)

        each(ranks, collect, rank + 1)

        @pl.when(rank < ranks - 1)
        def _():
            for i in range(H):
                grim_copy(i).wait_recv()
                for which in range(2):
                    tail[i, which] = tail[i, which] + rrim[i, which].astype(f32)

        for p in range(2):
            for which in range(2):
                put_copy(H - 2 + p, which).wait()
        for i in range(H):
            cols = slice((i % half) * HD, (i % half + 1) * HD)
            for which, held in enumerate((gk, gv)):
                cut = BLOCK - SUMMARY
                tail[i, which, cut:, :] = tail[i, which, cut:, :] + acc[i // half, which, :, cols]
                held[i // 7, pl.ds(i % 7 * BLOCK, BLOCK), :] = tail[i, which].astype(bf16)
        ends = [
            pltpu.make_async_copy(
                held.at[i // 7, pl.ds(i % 7 * BLOCK, BLOCK), :],
                out.at[pl.ds(last, BLOCK), pl.ds(i * HD, HD)],
                loc.at[2 + i * 2 + which],
            )
            for i in range(H)
            for which, (held, out) in enumerate(((gk, gk_out), (gv, gv_out)))
        ]
        for copy in ends:
            copy.start()

        others(pairs, pair, lambda p: pair_copy(p, pair).wait_recv())
        total = gall[0]
        for p in range(1, gall.shape[0]):
            total = total + gall[p]
        gain_out[...] = total * (dps * ranks * length) ** -0.5

        others(pairs, pair, lambda p: pair_copy(pair, p).wait_send())
        each(ranks, lambda t: sum_copy(rank, t).wait_send(), rank + 1)

        @pl.when(rank < ranks - 1)
        def _():
            for i in range(H):
                for which in range(2):
                    rim_copy(i, which).wait_send()

        @pl.when(rank > 0)
        def _():
            for i in range(H):
                grim_copy(i).wait_send()

        for p in range(PARTS):
            each(rank, lambda t, p=p: gsum_copy(p, rank, t).wait_send())
        for copy in ends:
            copy.wait()


def solution(mesh):
    dps, ranks = mesh.shape["dp"], mesh.shape["ctx"]

    def per_device(queries, keys, values, cotangent, gain):
        _, length, width = queries.shape
        flat = lambda x: x.reshape(length, width)
        q, k, v, do = flat(queries), flat(keys), flat(values), flat(cotangent)
        col = lambda rows: pl.BlockSpec((rows, HD), lambda h: (0, h))
        away = pl.BlockSpec(memory_space=pl.ANY)
        half = H // PARTS
        last = length - BLOCK
        big = jax.ShapeDtypeStruct((length, width), bf16)
        dma = lambda *shape: pltpu.SemaphoreType.DMA(shape)
        out = pl.pallas_call(
            exchange_kernel,
            name="attend_exchange",
            grid=(H,),
            in_specs=[col(length)] * 4 + [col(1), away, away],
            out_specs=[col(length), col(length), away, away, pl.BlockSpec((H, HD), lambda h: (0, 0))],
            out_shape=[big] * 4 + [jax.ShapeDtypeStruct((H, HD), f32)],
            scratch_shapes=[
                pltpu.VMEM((H, 2, BLOCK, HD), bf16),
                pltpu.VMEM((2, SUMMARY, width), bf16),
                pltpu.VMEM((ranks, 2, SUMMARY, width), bf16),
                pltpu.VMEM((H, 2, BLOCK, HD), bf16),
                pltpu.VMEM((H, 2, BLOCK, HD), bf16),
                pltpu.VMEM((PARTS, ranks, 2, SUMMARY, half * HD), bf16),
                pltpu.VMEM((PARTS, ranks, 2, SUMMARY, half * HD), bf16),
                pltpu.VMEM((2, last, HD), bf16),
                pltpu.VMEM((2, last, HD), bf16),
                pltpu.VMEM((H, 2, BLOCK, HD), f32),
                pltpu.VMEM((PARTS, 2, SUMMARY, half * HD), f32),
                pltpu.VMEM((H, HD), f32),
                pltpu.VMEM((dps * 2, H, HD), f32),
                pltpu.VMEM((ranks // 2, H, HD), f32),
                dma(H, 2), dma(H, 2),
                dma(ranks), dma(ranks),
                dma(H), dma(H),
                dma(PARTS, ranks), dma(PARTS, ranks),
                dma(dps * 2), dma(dps * 2),
                dma(ranks // 2), dma(ranks // 2),
                dma(2 + 2 * H), dma(2, 2),
            ],
            compiler_params=pltpu.CompilerParams(
                collective_id=0, has_side_effects=True, vmem_limit_bytes=48 << 20
            ),
        )(q, do, k, v, gain.reshape(1, width), k, v)
        whole = lambda x: x.reshape(1, length, width)
        return whole(out[0]), whole(out[1]), whole(out[2]), whole(out[3]), out[4].reshape(width)

    spread = P("dp", "ctx", None)
    return jax.shard_map(
        per_device,
        mesh=mesh,
        in_specs=(spread,) * 4 + (P(),),
        out_specs=(spread,) * 4 + (P(),),
        check_vma=False,
    )
```

```python
import jax
import jax.numpy as jnp
from jax import lax
from jax.experimental import pallas as pl
from jax.experimental.pallas import tpu as pltpu
from jax.sharding import PartitionSpec as P

f32 = jnp.float32
bf16 = jnp.bfloat16
MESH = pl.DeviceIdType.MESH

H = 8
HD = 128
BLOCK = 128
STRIDE = 1024
SUMMARY = 8
SCALE = HD**-0.5
LOG2E = 1.4426950408889634
NEG = -1e30
TILE = 256
OUTWARD = (0, 1, 3, 8)
BACK = (0, 5, 7, 8)


def nt(a, b):
    return lax.dot_general(a, b, (((1,), (1,)), ((), ())), preferred_element_type=f32)


def nn(a, b):
    return lax.dot_general(a, b, (((1,), (0,)), ((), ())), preferred_element_type=f32)


def attend_head(rank, q_ref, do_ref, kx, vx, sk, sv, gain, o_ref, gq_ref, gk_ref, gv_ref):
    length = q_ref.shape[0]
    blocks = length // BLOCK
    nb = TILE // BLOCK
    slots = sk.shape[0]
    skT, svT, kxT, vxT = sk.T, sv.T, kx.T, vx.T
    before = lax.broadcasted_iota(jnp.int32, (BLOCK, BLOCK), 0) > lax.broadcasted_iota(
        jnp.int32, (BLOCK, BLOCK), 1
    )
    dk, dv = [None] * (blocks + 1), [None] * (blocks + 1)
    dsk = dsv = gp = None
    plus = lambda old, new: new if old is None else old + new
    none = jnp.zeros((BLOCK, BLOCK), bf16)

    for t in range(length // TILE):
        rows = pl.ds(t * TILE, TILE)
        first = t * nb
        near = slice(first * BLOCK, (first + nb + 1) * BLOCK)
        qf = q_ref[rows, :].astype(f32)
        qs = (qf * gain).astype(bf16)
        do = do_ref[rows, :]

        def band(full, start):
            columns = []
            for i in range(nb):
                lanes = slice(i * BLOCK, (i + 1) * BLOCK)
                earlier = full[i * BLOCK : (i + 1) * BLOCK, lanes]
                if start is not None and t == 0 and i == 0:
                    earlier = jnp.where(rank > 0, earlier, start)
                columns.append(jnp.where(before, earlier, full[(i + 1) * BLOCK : (i + 2) * BLOCK, lanes]))
            return jnp.concatenate(columns, 1)

        sb = band(nt(kx[near], qs), NEG)
        db = band(nt(vx[near], do), None)
        ss = nt(sk, qs)
        ds = nt(sv, do)
        slot = lax.broadcasted_iota(jnp.int32, (slots, TILE), 0)
        if t == 0:
            spos = slot // SUMMARY * STRIDE + STRIDE - SUMMARY + slot % SUMMARY
            qpos = rank * length + lax.broadcasted_iota(jnp.int32, (slots, TILE), 1)
            seen = qpos - spos >= BLOCK
        else:
            seen = slot < SUMMARY * rank
        ss = jnp.where(seen, ss, NEG)
        top = jnp.maximum(jnp.max(sb, 0, keepdims=True), jnp.max(ss, 0, keepdims=True))
        eb = jnp.exp2((sb - top) * (SCALE * LOG2E))
        es = jnp.exp2((ss - top) * (SCALE * LOG2E))
        inv = 1.0 / (jnp.sum(eb, 0, keepdims=True) + jnp.sum(es, 0, keepdims=True))
        pb, ps = eb * inv, es * inv
        delta = jnp.sum(pb * db, 0, keepdims=True) + jnp.sum(ps * ds, 0, keepdims=True)
        gb = pb * ((db - delta) * SCALE)
        gs = ps * ((ds - delta) * SCALE)

        def unfold(x, xs):
            strips = []
            for j in range(nb + 1):
                cells = []
                for i in range(nb):
                    cell = x[:, i * BLOCK : (i + 1) * BLOCK]
                    if j == i:
                        cells.append(jnp.where(before, cell, 0.0).astype(bf16))
                    elif j == i + 1:
                        cells.append(jnp.where(before, 0.0, cell).astype(bf16))
                    else:
                        cells.append(none)
                strips.append(jnp.concatenate(cells, 1))
            return jnp.concatenate(strips + [xs.astype(bf16)], 0)

        prob, dscore = unfold(pb, ps), unfold(gb, gs)
        dvt, dkt = nn(prob, do), nn(dscore, qs)
        for j in range(nb + 1):
            strip = slice(j * BLOCK, (j + 1) * BLOCK)
            dv[first + j] = plus(dv[first + j], dvt[strip])
            dk[first + j] = plus(dk[first + j], dkt[strip])
        dsv = plus(dsv, dvt[(nb + 1) * BLOCK :])
        dsk = plus(dsk, dkt[(nb + 1) * BLOCK :])
        o_ref[rows, :] = nn(jnp.concatenate([vxT[:, near], svT], 1), prob).T.astype(bf16)
        dq = nn(jnp.concatenate([kxT[:, near], skT], 1), dscore).T
        gq_ref[rows, :] = (dq * gain).astype(bf16)
        gp = plus(gp, jnp.sum(dq * qf, 0, keepdims=True))
        for j in range(nb):
            n = first + j
            if n > 0:
                gk_ref[pl.ds((n - 1) * BLOCK, BLOCK), :] = dk[n].astype(bf16)
                gv_ref[pl.ds((n - 1) * BLOCK, BLOCK), :] = dv[n].astype(bf16)
    return dk[0], dv[0], dk[blocks], dv[blocks], dsk, dsv, gp


def exchange_kernel(
    q_ref, do_ref, k_ref, v_ref, g_ref, k_all, v_all,
    o_ref, gq_ref, gk_ref, gv_ref, ends_ref, gain_out,
    rim, mine, sums, grim, rrim, gsum, rsum, tail, acc, gbuf, gsub, gall,
    rim_s, rim_r, sum_s, sum_r, grim_s, grim_r, gsum_s, gsum_r, ga_s, ga_r, gb_s, gb_r, loc,
):
    h = pl.program_id(0)
    dp, rank = lax.axis_index("dp"), lax.axis_index("ctx")
    dps, ranks = lax.axis_size("dp"), lax.axis_size("ctx")
    length = q_ref.shape[0]
    last = length - BLOCK
    pair, side = rank // 2, rank % 2
    cell, cells = dp * 2 + side, dps * 2
    pairs = ranks // 2
    groups, parts = len(OUTWARD) - 1, len(BACK) - 1

    def heads(edges, i):
        return pl.ds(edges[i] * HD, (edges[i + 1] - edges[i]) * HD)

    def rim_copy(i, which):
        src = (k_all, v_all)[which].at[pl.ds(last, BLOCK), pl.ds(pl.multiple_of(i * HD, HD), HD)]
        return pltpu.make_async_remote_copy(
            src, rim.at[i, which], rim_s.at[i, which], rim_r.at[i, which],
            device_id={"ctx": jnp.minimum(rank + 1, ranks - 1)}, device_id_type=MESH,
        )

    def sum_copy(group, source, target):
        lanes = heads(OUTWARD, group)
        return pltpu.make_async_remote_copy(
            mine.at[:, :, lanes], sums.at[source, :, :, lanes], sum_s.at[group, target], sum_r.at[group, source],
            device_id={"ctx": target}, device_id_type=MESH,
        )

    def grim_copy(i):
        return pltpu.make_async_remote_copy(
            grim.at[i], rrim.at[i], grim_s.at[i], grim_r.at[i],
            device_id={"ctx": jnp.maximum(rank - 1, 0)}, device_id_type=MESH,
        )

    def gsum_copy(part, source, target):
        lanes = heads(BACK, part)
        return pltpu.make_async_remote_copy(
            gsum.at[target, :, :, lanes], rsum.at[source, :, :, lanes],
            gsum_s.at[part, target], gsum_r.at[part, source],
            device_id={"ctx": target}, device_id_type=MESH,
        )

    def cell_copy(source, target):
        return pltpu.make_async_remote_copy(
            gbuf, gsub.at[source], ga_s.at[target], ga_r.at[source],
            device_id={"dp": target // 2, "ctx": pair * 2 + target % 2}, device_id_type=MESH,
        )

    def pair_copy(source, target):
        return pltpu.make_async_remote_copy(
            gsub.at[cell], gall.at[source], gb_s.at[target], gb_r.at[source],
            device_id={"ctx": target * 2 + side}, device_id_type=MESH,
        )

    def each(count, body, start=0):
        lax.fori_loop(start, count, lambda i, c: (body(i), c)[1], 0)

    def send_rim(i):
        @pl.when(rank < ranks - 1)
        def _():
            for which in range(2):
                rim_copy(i, which).start()

    def send_sums(group):
        each(ranks, lambda t: sum_copy(group, rank, t).start(), rank + 1)

    @pl.when(h == 0)
    def _():
        own = [
            pltpu.make_async_copy(full.at[pl.ds(length - SUMMARY, SUMMARY), :], mine.at[i], loc.at[i])
            for i, full in enumerate((k_all, v_all))
        ]
        for copy in own:
            copy.start()
        barrier = pltpu.get_barrier_semaphore()

        def greet_rank(t):
            @pl.when(t != rank)
            def _():
                pl.semaphore_signal(barrier, inc=1, device_id={"ctx": t}, device_id_type=MESH)

        def greet_cell(c):
            @pl.when(c // 2 != dp)
            def _():
                pl.semaphore_signal(
                    barrier, inc=1, device_id={"dp": c // 2, "ctx": pair * 2 + c % 2}, device_id_type=MESH
                )

        each(ranks, greet_rank)
        each(cells, greet_cell)
        for copy in own:
            copy.wait()
        pl.semaphore_wait(barrier, ranks - 1 + cells - 2)
        send_rim(0)
        send_sums(0)
        send_rim(1)
        send_sums(1)

    @pl.when(h == 1)
    def _():
        send_rim(2)
        for group in range(2, groups):
            send_sums(group)

    @pl.when((h >= 1) & (h + 2 < H))
    def _():
        send_rim(h + 2)

    for group in range(groups):

        @pl.when(h == OUTWARD[group])
        def _(group=group):
            each(rank, lambda s: sum_copy(group, s, rank).wait_recv())

    @pl.when(rank > 0)
    def _():
        for which in range(2):
            rim_copy(h, which).wait_recv()

    lanes = pl.ds(pl.multiple_of(h * HD, HD), HD)
    slots = sums.shape[0] * SUMMARY
    there = lax.broadcasted_iota(jnp.int32, (slots, HD), 0) < SUMMARY * rank

    def summary(which):
        rows = sums[:, which, :, lanes].astype(f32).reshape(slots, HD)
        return jnp.where(there, rows, 0.0).astype(bf16)

    def extended(which, ref):
        edge = jnp.where(rank > 0, rim[h, which], jnp.zeros((BLOCK, HD), bf16))
        return jnp.concatenate([edge, ref[...]], 0)

    dk0, dv0, dkn, dvn, dsk, dsv, gp = attend_head(
        rank, q_ref, do_ref, extended(0, k_ref), extended(1, v_ref), summary(0), summary(1), g_ref[...],
        o_ref, gq_ref, gk_ref, gv_ref,
    )
    grim[h, 0] = dk0.astype(bf16)
    grim[h, 1] = dv0.astype(bf16)
    tail[h, 0] = dkn
    tail[h, 1] = dvn
    gsum[:, 0, :, lanes] = dsk.reshape(slots // SUMMARY, SUMMARY, HD).astype(bf16)
    gsum[:, 1, :, lanes] = dsv.reshape(slots // SUMMARY, SUMMARY, HD).astype(bf16)
    gbuf[pl.ds(h, 1), :] = gp

    @pl.when(h == H - 1)
    def _():
        each(cells, lambda c: pl.when(c != cell)(lambda: cell_copy(cell, c).start()))

    @pl.when(rank > 0)
    def _():
        grim_copy(h).start()

    for part in range(parts):

        @pl.when(h == BACK[part + 1] - 1)
        def _(part=part):
            each(rank, lambda t: gsum_copy(part, rank, t).start())

    @pl.when(h == H - 1)
    def _():
        def others(count, me, body):
            each(count, lambda i: pl.when(i != me)(lambda: body(i)))

        others(cells, cell, lambda c: cell_copy(c, cell).wait_recv())
        gsub[cell] = gbuf[...]
        total = gsub[0]
        for c in range(1, gsub.shape[0]):
            total = total + gsub[c]
        gsub[cell] = total
        gall[pair] = total
        others(pairs, pair, lambda p: pair_copy(pair, p).start())

        acc[...] = jnp.zeros(acc.shape, f32)

        def collect(s):
            for part in range(parts):
                gsum_copy(part, s, rank).wait_recv()
            acc[...] = acc[...] + rsum[s].astype(f32)

        each(ranks, collect, rank + 1)

        @pl.when(rank < ranks - 1)
        def _():
            for i in range(H):
                grim_copy(i).wait_recv()
                for which in range(2):
                    tail[i, which] = tail[i, which] + rrim[i, which].astype(f32)

        cut = BLOCK - SUMMARY
        for i in range(H):
            cols = slice(i * HD, (i + 1) * HD)
            for which in range(2):
                tail[i, which, cut:, :] = tail[i, which, cut:, :] + acc[which, :, cols]
                ends_ref[which, :, cols] = tail[i, which].astype(bf16)

        others(pairs, pair, lambda p: pair_copy(p, pair).wait_recv())
        total = gall[0]
        for p in range(1, gall.shape[0]):
            total = total + gall[p]
        gain_out[...] = total * (dps * ranks * length) ** -0.5

        others(cells, cell, lambda c: cell_copy(cell, c).wait_send())
        others(pairs, pair, lambda p: pair_copy(pair, p).wait_send())
        for group in range(groups):
            each(ranks, lambda t, group=group: sum_copy(group, rank, t).wait_send(), rank + 1)

        @pl.when(rank < ranks - 1)
        def _():
            for i in range(H):
                for which in range(2):
                    rim_copy(i, which).wait_send()

        @pl.when(rank > 0)
        def _():
            for i in range(H):
                grim_copy(i).wait_send()

        for part in range(parts):
            each(rank, lambda t, part=part: gsum_copy(part, rank, t).wait_send())


def write_kernel(o_in, gq_in, gk_in, gv_in, ends_in, gain_in, o_out, gq_out, gk_out, gv_out, gain_out, sems):
    last = gk_in.shape[0]
    length = o_in.shape[0]
    moves = []
    for source, target in ((o_in, o_out), (gq_in, gq_out)):
        for i in range(2):
            rows = pl.ds(i * (length // 2), length // 2)
            moves.append((source.at[rows], target.at[rows]))
    for which, (source, target) in enumerate(((gk_in, gk_out), (gv_in, gv_out))):
        for i in range(2):
            rows = pl.ds(i * (last // 2), last // 2)
            moves.append((source.at[rows], target.at[rows]))
        moves.append((ends_in.at[which], target.at[pl.ds(last, length - last)]))
    copies = [pltpu.make_async_copy(a, b, sems.at[i]) for i, (a, b) in enumerate(moves)]
    for copy in copies:
        copy.start()
    for i in range(H):
        gain_out[:, i * HD : (i + 1) * HD] = gain_in[i : i + 1, :]
    for copy in copies:
        copy.wait()


def solution(mesh):
    dps, ranks = mesh.shape["dp"], mesh.shape["ctx"]

    def per_device(queries, keys, values, cotangent, gain):
        _, length, width = queries.shape
        flat = lambda x: x.reshape(length, width)
        q, k, v, do = flat(queries), flat(keys), flat(values), flat(cotangent)
        col = lambda rows: pl.BlockSpec((rows, HD), lambda h: (0, h))
        away = pl.BlockSpec(memory_space=pl.ANY)
        last = length - BLOCK
        like = jax.ShapeDtypeStruct
        dma = lambda *shape: pltpu.SemaphoreType.DMA(shape)
        groups, parts = len(OUTWARD) - 1, len(BACK) - 1
        held = pl.pallas_call(
            exchange_kernel,
            name="attend_exchange",
            grid=(H,),
            in_specs=[col(length)] * 4 + [col(1), away, away],
            out_specs=[col(length)] * 2
            + [col(last)] * 2
            + [pl.BlockSpec((2, BLOCK, width), lambda h: (0, 0, 0)), pl.BlockSpec((H, HD), lambda h: (0, 0))],
            out_shape=[like((length, width), bf16)] * 2
            + [like((last, width), bf16)] * 2
            + [like((2, BLOCK, width), bf16), like((H, HD), f32)],
            scratch_shapes=[
                pltpu.VMEM((H, 2, BLOCK, HD), bf16),
                pltpu.VMEM((2, SUMMARY, width), bf16),
                pltpu.VMEM((ranks, 2, SUMMARY, width), bf16),
                pltpu.VMEM((H, 2, BLOCK, HD), bf16),
                pltpu.VMEM((H, 2, BLOCK, HD), bf16),
                pltpu.VMEM((ranks, 2, SUMMARY, width), bf16),
                pltpu.VMEM((ranks, 2, SUMMARY, width), bf16),
                pltpu.VMEM((H, 2, BLOCK, HD), f32),
                pltpu.VMEM((2, SUMMARY, width), f32),
                pltpu.VMEM((H, HD), f32),
                pltpu.VMEM((dps * 2, H, HD), f32),
                pltpu.VMEM((ranks // 2, H, HD), f32),
                dma(H, 2), dma(H, 2),
                dma(groups, ranks), dma(groups, ranks),
                dma(H), dma(H),
                dma(parts, ranks), dma(parts, ranks),
                dma(dps * 2), dma(dps * 2),
                dma(ranks // 2), dma(ranks // 2),
                dma(2),
            ],
            compiler_params=pltpu.CompilerParams(
                collective_id=0, has_side_effects=True, vmem_limit_bytes=44 << 20
            ),
        )(q, do, k, v, gain.reshape(1, width), k, v)
        one = pl.BlockSpec(memory_space=pltpu.VMEM)
        out = pl.pallas_call(
            write_kernel,
            name="attend_write",
            in_specs=[away] * 5 + [one],
            out_specs=[away] * 4 + [one],
            out_shape=[like((length, width), bf16)] * 4 + [like((1, width), f32)],
            scratch_shapes=[dma(10)],
            compiler_params=pltpu.CompilerParams(vmem_limit_bytes=2 << 20),
        )(*held)
        whole = lambda x: x.reshape(1, length, width)
        return whole(out[0]), whole(out[1]), whole(out[2]), whole(out[3]), out[4].reshape(width)

    spread = P("dp", "ctx", None)
    return jax.shard_map(
        per_device,
        mesh=mesh,
        in_specs=(spread,) * 4 + (P(),),
        out_specs=(spread,) * 4 + (P(),),
        check_vma=False,
    )
```

```python
import jax
import jax.numpy as jnp
from jax import lax
from jax.experimental import pallas as pl
from jax.experimental.pallas import tpu as pltpu
from jax.sharding import PartitionSpec as P

f32 = jnp.float32
bf16 = jnp.bfloat16
MESH = pl.DeviceIdType.MESH

H = 8
HD = 128
BLOCK = 128
STRIDE = 1024
SUMMARY = 8
SCALE = HD**-0.5
LOG2E = 1.4426950408889634
NEG = -1e30
TILE = 256
OUTWARD = (0, 1, 3, 5, 8)
BACK = (0, 2, 4, 6, 7, 8)
EARLY = 3


def nt(a, b):
    return lax.dot_general(a, b, (((1,), (1,)), ((), ())), preferred_element_type=f32)


def nn(a, b):
    return lax.dot_general(a, b, (((1,), (0,)), ((), ())), preferred_element_type=f32)


def attend_head(rank, q_ref, do_ref, kx, vx, sk, sv, gain, o_ref, gq_ref, gk_ref, gv_ref):
    length = q_ref.shape[0]
    blocks = length // BLOCK
    nb = TILE // BLOCK
    slots = sk.shape[0]
    skT, svT, kxT, vxT = sk.T, sv.T, kx.T, vx.T
    before = lax.broadcasted_iota(jnp.int32, (BLOCK, BLOCK), 0) > lax.broadcasted_iota(
        jnp.int32, (BLOCK, BLOCK), 1
    )
    dk, dv = [None] * (blocks + 1), [None] * (blocks + 1)
    dsk = dsv = gp = None
    plus = lambda old, new: new if old is None else old + new
    none = jnp.zeros((BLOCK, BLOCK), bf16)

    for t in range(length // TILE):
        rows = pl.ds(t * TILE, TILE)
        first = t * nb
        near = slice(first * BLOCK, (first + nb + 1) * BLOCK)
        qf = q_ref[rows, :].astype(f32)
        qs = (qf * gain).astype(bf16)
        do = do_ref[rows, :]

        def band(full, start):
            columns = []
            for i in range(nb):
                lanes = slice(i * BLOCK, (i + 1) * BLOCK)
                earlier = full[i * BLOCK : (i + 1) * BLOCK, lanes]
                if start is not None and t == 0 and i == 0:
                    earlier = jnp.where(rank > 0, earlier, start)
                columns.append(jnp.where(before, earlier, full[(i + 1) * BLOCK : (i + 2) * BLOCK, lanes]))
            return jnp.concatenate(columns, 1)

        sb = band(nt(kx[near], qs), NEG)
        db = band(nt(vx[near], do), None)
        ss = nt(sk, qs)
        ds = nt(sv, do)
        slot = lax.broadcasted_iota(jnp.int32, (slots, TILE), 0)
        if t == 0:
            spos = slot // SUMMARY * STRIDE + STRIDE - SUMMARY + slot % SUMMARY
            qpos = rank * length + lax.broadcasted_iota(jnp.int32, (slots, TILE), 1)
            seen = qpos - spos >= BLOCK
        else:
            seen = slot < SUMMARY * rank
        ss = jnp.where(seen, ss, NEG)
        top = jnp.maximum(jnp.max(sb, 0, keepdims=True), jnp.max(ss, 0, keepdims=True))
        eb = jnp.exp2((sb - top) * (SCALE * LOG2E))
        es = jnp.exp2((ss - top) * (SCALE * LOG2E))
        inv = 1.0 / (jnp.sum(eb, 0, keepdims=True) + jnp.sum(es, 0, keepdims=True))
        pb, ps = eb * inv, es * inv
        delta = jnp.sum(pb * db, 0, keepdims=True) + jnp.sum(ps * ds, 0, keepdims=True)
        gb = pb * ((db - delta) * SCALE)
        gs = ps * ((ds - delta) * SCALE)

        def unfold(x, xs):
            strips = []
            for j in range(nb + 1):
                cells = []
                for i in range(nb):
                    cell = x[:, i * BLOCK : (i + 1) * BLOCK]
                    if j == i:
                        cells.append(jnp.where(before, cell, 0.0).astype(bf16))
                    elif j == i + 1:
                        cells.append(jnp.where(before, 0.0, cell).astype(bf16))
                    else:
                        cells.append(none)
                strips.append(jnp.concatenate(cells, 1))
            return jnp.concatenate(strips + [xs.astype(bf16)], 0)

        prob, dscore = unfold(pb, ps), unfold(gb, gs)
        dvt, dkt = nn(prob, do), nn(dscore, qs)
        for j in range(nb + 1):
            strip = slice(j * BLOCK, (j + 1) * BLOCK)
            dv[first + j] = plus(dv[first + j], dvt[strip])
            dk[first + j] = plus(dk[first + j], dkt[strip])
        dsv = plus(dsv, dvt[(nb + 1) * BLOCK :])
        dsk = plus(dsk, dkt[(nb + 1) * BLOCK :])
        o_ref[rows, :] = nn(jnp.concatenate([vxT[:, near], svT], 1), prob).T.astype(bf16)
        dq = nn(jnp.concatenate([kxT[:, near], skT], 1), dscore).T
        gq_ref[rows, :] = (dq * gain).astype(bf16)
        gp = plus(gp, jnp.sum(dq * qf, 0, keepdims=True))
        for j in range(nb):
            n = first + j
            if n > 0:
                gk_ref[pl.ds((n - 1) * BLOCK, BLOCK), :] = dk[n].astype(bf16)
                gv_ref[pl.ds((n - 1) * BLOCK, BLOCK), :] = dv[n].astype(bf16)
    return dk[0], dv[0], dk[blocks], dv[blocks], dsk, dsv, gp


def exchange_kernel(
    q_ref, do_ref, k_ref, v_ref, g_ref, k_all, v_all,
    o_ref, gq_ref, gk_ref, gv_ref, ends_ref, gain_out,
    rim, sums, grim, rrim, gsum, rsum, tail, acc, racc, gbuf, gsub, gall,
    rim_s, rim_r, part_s, part_r, sum_s, sum_r, grim_s, grim_r, gsum_s, gsum_r, gpart_s, gpart_r,
    ga_s, ga_r, gb_s, gb_r, loc,
):
    h = pl.program_id(0)
    dp, rank = lax.axis_index("dp"), lax.axis_index("ctx")
    dps, ranks = lax.axis_size("dp"), lax.axis_size("ctx")
    length = q_ref.shape[0]
    last = length - BLOCK
    pair, side = rank // 2, rank % 2
    partner = pair * 2 + 1 - side
    cell, cells = dp * 2 + side, dps * 2
    pairs = ranks // 2
    groups, parts = len(OUTWARD) - 1, len(BACK) - 1

    def heads(edges, i, j=None):
        j = i + 1 if j is None else j
        return pl.ds(edges[i] * HD, (edges[j] - edges[i]) * HD)

    def rim_copy(i, which):
        src = (k_all, v_all)[which].at[pl.ds(last, BLOCK), pl.ds(pl.multiple_of(i * HD, HD), HD)]
        return pltpu.make_async_remote_copy(
            src, rim.at[i, which], rim_s.at[i, which], rim_r.at[i, which],
            device_id={"ctx": jnp.minimum(rank + 1, ranks - 1)}, device_id_type=MESH,
        )

    def part_copy(source):
        return pltpu.make_async_remote_copy(
            sums.at[source], sums.at[source], part_s, part_r, device_id={"ctx": partner}, device_id_type=MESH
        )

    def sum_copy(group, source, target):
        both, lanes = pl.ds(source * 2, 2), heads(OUTWARD, group)
        return pltpu.make_async_remote_copy(
            sums.at[both, :, :, lanes], sums.at[both, :, :, lanes], sum_s.at[group, target], sum_r.at[group, source],
            device_id={"ctx": target * 2 + side}, device_id_type=MESH,
        )

    def grim_copy(i):
        return pltpu.make_async_remote_copy(
            grim.at[i], rrim.at[i], grim_s.at[i], grim_r.at[i],
            device_id={"ctx": jnp.maximum(rank - 1, 0)}, device_id_type=MESH,
        )

    def gsum_copy(part, source, target):
        lanes = heads(BACK, part)
        return pltpu.make_async_remote_copy(
            gsum.at[pl.ds(target * 2, 2), :, :, lanes], rsum.at[source, :, :, :, lanes],
            gsum_s.at[part, target], gsum_r.at[part, source],
            device_id={"ctx": target * 2 + side}, device_id_type=MESH,
        )

    def gpart_copy(late):
        lanes = heads(BACK, EARLY, parts) if late else heads(BACK, 0, EARLY)
        return pltpu.make_async_remote_copy(
            acc.at[1 - side, :, :, lanes], racc.at[:, :, lanes], gpart_s.at[late], gpart_r.at[late],
            device_id={"ctx": partner}, device_id_type=MESH,
        )

    def cell_copy(source, target):
        return pltpu.make_async_remote_copy(
            gbuf, gsub.at[source], ga_s.at[target], ga_r.at[source],
            device_id={"dp": target // 2, "ctx": pair * 2 + target % 2}, device_id_type=MESH,
        )

    def pair_copy(source, target):
        return pltpu.make_async_remote_copy(
            gsub.at[cell], gall.at[source], gb_s.at[target], gb_r.at[source],
            device_id={"ctx": target * 2 + side}, device_id_type=MESH,
        )

    def each(count, body, start=0):
        lax.fori_loop(start, count, lambda i, c: (body(i), c)[1], 0)

    def others(count, me, body):
        each(count, lambda i: pl.when(i != me)(lambda: body(i)))

    def send_rim(i):
        @pl.when(rank < ranks - 1)
        def _():
            for which in range(2):
                rim_copy(i, which).start()

    def send_sums(group):
        each(pairs, lambda t: sum_copy(group, pair, t).start(), pair + 1)

    def collect(some, lanes):
        acc[:, :, :, lanes] = gsum[pl.ds(pair * 2, 2), :, :, lanes].astype(f32)

        def add(s):
            for part in some:
                gsum_copy(part, s, pair).wait_recv()
            acc[:, :, :, lanes] = acc[:, :, :, lanes] + rsum[s, :, :, :, lanes].astype(f32)

        each(pairs, add, pair + 1)

    def close(i):
        @pl.when(rank < ranks - 1)
        def _():
            grim_copy(i).wait_recv()
            for which in range(2):
                tail[i, which] = tail[i, which] + rrim[i, which].astype(f32)

        for which in range(2):
            ends_ref[which, :, i * HD : (i + 1) * HD] = tail[i, which].astype(bf16)

    @pl.when(h == 0)
    def _():
        own = [
            pltpu.make_async_copy(
                full.at[pl.ds(length - SUMMARY, SUMMARY), :], sums.at[rank, i], loc.at[i]
            )
            for i, full in enumerate((k_all, v_all))
        ]
        for copy in own:
            copy.start()
        barrier = pltpu.get_barrier_semaphore()

        def greet(**device):
            pl.semaphore_signal(barrier, inc=1, device_id=device, device_id_type=MESH)

        others(pairs, pair, lambda p: greet(ctx=p * 2 + side))
        others(cells, cell, lambda c: greet(dp=c // 2, ctx=pair * 2 + c % 2))
        beside = rank + 2 * side - 1
        inside = (beside >= 0) & (beside < ranks)

        @pl.when(inside)
        def _():
            greet(ctx=jnp.clip(beside, 0, ranks - 1))

        for copy in own:
            copy.wait()
        pl.semaphore_wait(barrier, pairs - 1 + cells - 1 + inside.astype(jnp.int32))
        part_copy(rank).start()
        send_rim(0)
        part_copy(partner).wait_recv()
        send_sums(0)
        send_sums(1)
        send_rim(1)

    @pl.when(h == 1)
    def _():
        send_rim(2)
        for group in range(2, groups):
            send_sums(group)

    @pl.when((h >= 1) & (h + 2 < H))
    def _():
        send_rim(h + 2)

    for group in range(groups):

        @pl.when(h == OUTWARD[group])
        def _(group=group):
            each(pair, lambda s: sum_copy(group, s, pair).wait_recv())

    @pl.when(rank > 0)
    def _():
        for which in range(2):
            rim_copy(h, which).wait_recv()

    lanes = pl.ds(pl.multiple_of(h * HD, HD), HD)
    slots = sums.shape[0] * SUMMARY
    there = lax.broadcasted_iota(jnp.int32, (slots, HD), 0) < SUMMARY * rank

    def summary(which):
        rows = sums[:, which, :, lanes].astype(f32).reshape(slots, HD)
        return jnp.where(there, rows, 0.0).astype(bf16)

    def extended(which, ref):
        edge = jnp.where(rank > 0, rim[h, which], jnp.zeros((BLOCK, HD), bf16))
        return jnp.concatenate([edge, ref[...]], 0)

    dk0, dv0, dkn, dvn, dsk, dsv, gp = attend_head(
        rank, q_ref, do_ref, extended(0, k_ref), extended(1, v_ref), summary(0), summary(1), g_ref[...],
        o_ref, gq_ref, gk_ref, gv_ref,
    )
    grim[h, 0] = dk0.astype(bf16)
    grim[h, 1] = dv0.astype(bf16)
    tail[h, 0] = dkn
    tail[h, 1] = dvn
    gsum[:, 0, :, lanes] = dsk.reshape(slots // SUMMARY, SUMMARY, HD).astype(bf16)
    gsum[:, 1, :, lanes] = dsv.reshape(slots // SUMMARY, SUMMARY, HD).astype(bf16)
    gbuf[pl.ds(h, 1), :] = gp

    @pl.when(rank > 0)
    def _():
        grim_copy(h).start()

    @pl.when(h == H - 1)
    def _():
        others(cells, cell, lambda c: cell_copy(cell, c).start())

    for part in range(parts):

        @pl.when(h == BACK[part + 1] - 1)
        def _(part=part):
            each(pair, lambda t: gsum_copy(part, pair, t).start())

    @pl.when(h == H - 2)
    def _():
        for group in range(groups):
            each(pairs, lambda t, group=group: sum_copy(group, pair, t).wait_send(), pair + 1)
        part_copy(rank).wait_send()

        @pl.when(rank < ranks - 1)
        def _():
            for i in range(H):
                for which in range(2):
                    rim_copy(i, which).wait_send()

        for i in range(H - 3):
            close(i)

    @pl.when(h == H - 1)
    def _():
        collect(range(EARLY), heads(BACK, 0, EARLY))
        gpart_copy(0).start()
        others(cells, cell, lambda c: cell_copy(c, cell).wait_recv())
        gsub[cell] = gbuf[...]
        total = gsub[0]
        for c in range(1, gsub.shape[0]):
            total = total + gsub[c]
        gsub[cell] = total
        gall[pair] = total
        others(pairs, pair, lambda p: pair_copy(pair, p).start())
        collect(range(EARLY, parts), heads(BACK, EARLY, parts))
        gpart_copy(1).start()
        for i in range(H - 3, H):
            close(i)
        for late in range(2):
            gpart_copy(late).wait_recv()
        for i in range(H):
            cols = slice(i * HD, (i + 1) * HD)
            for which in range(2):
                extra = acc[side, which, :, cols] + racc[which, :, cols]
                ends_ref[which, BLOCK - 16 :, cols] = (
                    tail[i, which, BLOCK - 16 :, :] + jnp.concatenate([jnp.zeros((16 - SUMMARY, HD), f32), extra], 0)
                ).astype(bf16)

        others(pairs, pair, lambda p: pair_copy(p, pair).wait_recv())
        total = gall[0]
        for p in range(1, gall.shape[0]):
            total = total + gall[p]
        gain_out[...] = total * (dps * ranks * length) ** -0.5

        others(cells, cell, lambda c: cell_copy(cell, c).wait_send())
        others(pairs, pair, lambda p: pair_copy(pair, p).wait_send())

        @pl.when(rank > 0)
        def _():
            for i in range(H):
                grim_copy(i).wait_send()

        for part in range(parts):
            each(pair, lambda t, part=part: gsum_copy(part, pair, t).wait_send())
        for late in range(2):
            gpart_copy(late).wait_send()


def write_kernel(o_in, gq_in, gk_in, gv_in, ends_in, gain_in, o_out, gq_out, gk_out, gv_out, gain_out, sems):
    last = gk_in.shape[0]
    length = o_in.shape[0]
    moves = []
    for source, target in ((o_in, o_out), (gq_in, gq_out)):
        for i in range(2):
            rows = pl.ds(i * (length // 2), length // 2)
            moves.append((source.at[rows], target.at[rows]))
    for which, (source, target) in enumerate(((gk_in, gk_out), (gv_in, gv_out))):
        for i in range(2):
            rows = pl.ds(i * (last // 2), last // 2)
            moves.append((source.at[rows], target.at[rows]))
        moves.append((ends_in.at[which], target.at[pl.ds(last, length - last)]))
    copies = [pltpu.make_async_copy(a, b, sems.at[i]) for i, (a, b) in enumerate(moves)]
    for copy in copies:
        copy.start()
    for i in range(H):
        gain_out[:, i * HD : (i + 1) * HD] = gain_in[i : i + 1, :]
    for copy in copies:
        copy.wait()


def solution(mesh):
    dps, ranks = mesh.shape["dp"], mesh.shape["ctx"]

    def per_device(queries, keys, values, cotangent, gain):
        _, length, width = queries.shape
        flat = lambda x: x.reshape(length, width)
        q, k, v, do = flat(queries), flat(keys), flat(values), flat(cotangent)
        col = lambda rows: pl.BlockSpec((rows, HD), lambda h: (0, h))
        away = pl.BlockSpec(memory_space=pl.ANY)
        last = length - BLOCK
        like = jax.ShapeDtypeStruct
        dma = lambda *shape: pltpu.SemaphoreType.DMA(shape)
        groups, parts = len(OUTWARD) - 1, len(BACK) - 1
        held = pl.pallas_call(
            exchange_kernel,
            name="attend_exchange",
            grid=(H,),
            in_specs=[col(length)] * 4 + [col(1), away, away],
            out_specs=[col(length)] * 2
            + [col(last)] * 2
            + [pl.BlockSpec((2, BLOCK, width), lambda h: (0, 0, 0)), pl.BlockSpec((H, HD), lambda h: (0, 0))],
            out_shape=[like((length, width), bf16)] * 2
            + [like((last, width), bf16)] * 2
            + [like((2, BLOCK, width), bf16), like((H, HD), f32)],
            scratch_shapes=[
                pltpu.VMEM((H, 2, BLOCK, HD), bf16),
                pltpu.VMEM((ranks, 2, SUMMARY, width), bf16),
                pltpu.VMEM((H, 2, BLOCK, HD), bf16),
                pltpu.VMEM((H, 2, BLOCK, HD), bf16),
                pltpu.VMEM((ranks, 2, SUMMARY, width), bf16),
                pltpu.VMEM((ranks // 2, 2, 2, SUMMARY, width), bf16),
                pltpu.VMEM((H, 2, BLOCK, HD), f32),
                pltpu.VMEM((2, 2, SUMMARY, width), f32),
                pltpu.VMEM((2, SUMMARY, width), f32),
                pltpu.VMEM((H, HD), f32),
                pltpu.VMEM((dps * 2, H, HD), f32),
                pltpu.VMEM((ranks // 2, H, HD), f32),
                dma(H, 2), dma(H, 2),
                pltpu.SemaphoreType.DMA, pltpu.SemaphoreType.DMA,
                dma(groups, ranks // 2), dma(groups, ranks // 2),
                dma(H), dma(H),
                dma(parts, ranks // 2), dma(parts, ranks // 2),
                dma(2), dma(2),
                dma(dps * 2), dma(dps * 2),
                dma(ranks // 2), dma(ranks // 2),
                dma(2),
            ],
            compiler_params=pltpu.CompilerParams(
                collective_id=0, has_side_effects=True, vmem_limit_bytes=44 << 20
            ),
        )(q, do, k, v, gain.reshape(1, width), k, v)
        one = pl.BlockSpec(memory_space=pltpu.VMEM)
        out = pl.pallas_call(
            write_kernel,
            name="attend_write",
            in_specs=[away] * 5 + [one],
            out_specs=[away] * 4 + [one],
            out_shape=[like((length, width), bf16)] * 4 + [like((1, width), f32)],
            scratch_shapes=[dma(10)],
            compiler_params=pltpu.CompilerParams(vmem_limit_bytes=2 << 20),
        )(*held)
        whole = lambda x: x.reshape(1, length, width)
        return whole(out[0]), whole(out[1]), whole(out[2]), whole(out[3]), out[4].reshape(width)

    spread = P("dp", "ctx", None)
    return jax.shard_map(
        per_device,
        mesh=mesh,
        in_specs=(spread,) * 4 + (P(),),
        out_specs=(spread,) * 4 + (P(),),
        check_vma=False,
    )
```

```python
import jax
import jax.numpy as jnp
from jax import lax
from jax.experimental import pallas as pl
from jax.experimental.pallas import tpu as pltpu
from jax.sharding import PartitionSpec as P

f32 = jnp.float32
bf16 = jnp.bfloat16
MESH = pl.DeviceIdType.MESH

H = 8
HD = 128
BLOCK = 128
STRIDE = 1024
SUMMARY = 8
SCALE = HD**-0.5
LOG2E = 1.4426950408889634
NEG = -1e30
TILE = 256
OUTWARD = (0, 1, 3, 8)
BACK = (0, 3, 6, 8)
EARLY = 2
AHEAD = 4


def nt(a, b):
    return lax.dot_general(a, b, (((1,), (1,)), ((), ())), preferred_element_type=f32)


def nn(a, b):
    return lax.dot_general(a, b, (((1,), (0,)), ((), ())), preferred_element_type=f32)


def plus(old, new):
    return new if old is None else old + new


def exchange_kernel(
    q_all, do_all, k_all, v_all, g_all,
    o_ref, gq_ref, gk_ref, gv_ref, gain_out,
    q, do, qs, kx, vx, g, sb, db, pst, gst, sums, grim, rrim, gsum, rsum, edge, acc, racc, gbuf, gsub, gall,
    rim_s, rim_r, part_s, part_r, sum_s, sum_r, grim_s, grim_r, gsum_s, gsum_r, gpart_s, gpart_r,
    ga_s, ga_r, gb_s, gb_r, loc, load,
):
    dp, rank = lax.axis_index("dp"), lax.axis_index("ctx")
    dps, ranks = lax.axis_size("dp"), lax.axis_size("ctx")
    length = q.shape[1]
    blocks = length // BLOCK
    last = length - BLOCK
    pair, side = rank // 2, rank % 2
    partner = pair * 2 + 1 - side
    cell, cells = dp * 2 + side, dps * 2
    pairs = ranks // 2
    groups, parts = len(OUTWARD) - 1, len(BACK) - 1

    def heads(edges, i, j=None):
        j = i + 1 if j is None else j
        return pl.ds(edges[i] * HD, (edges[j] - edges[i]) * HD)

    def rim_copy(i, which):
        src = (k_all, v_all)[which].at[pl.ds(last, BLOCK), pl.ds(pl.multiple_of(i * HD, HD), HD)]
        return pltpu.make_async_remote_copy(
            src, (kx, vx)[which].at[i, pl.ds(0, BLOCK), :], rim_s.at[i, which], rim_r.at[i, which],
            device_id={"ctx": jnp.minimum(rank + 1, ranks - 1)}, device_id_type=MESH,
        )

    def part_copy(source):
        return pltpu.make_async_remote_copy(
            sums.at[source], sums.at[source], part_s, part_r, device_id={"ctx": partner}, device_id_type=MESH
        )

    def sum_copy(group, source, target):
        both, lanes = pl.ds(source * 2, 2), heads(OUTWARD, group)
        return pltpu.make_async_remote_copy(
            sums.at[both, :, :, lanes], sums.at[both, :, :, lanes], sum_s.at[group, target], sum_r.at[group, source],
            device_id={"ctx": target * 2 + side}, device_id_type=MESH,
        )

    def grim_copy(i):
        return pltpu.make_async_remote_copy(
            grim.at[i], rrim.at[i], grim_s.at[i], grim_r.at[i],
            device_id={"ctx": jnp.maximum(rank - 1, 0)}, device_id_type=MESH,
        )

    def gsum_copy(part, source, target):
        lanes = heads(BACK, part)
        return pltpu.make_async_remote_copy(
            gsum.at[pl.ds(target * 2, 2), :, :, lanes], rsum.at[source, :, :, :, lanes],
            gsum_s.at[part, target], gsum_r.at[part, source],
            device_id={"ctx": target * 2 + side}, device_id_type=MESH,
        )

    def gpart_copy(late):
        lanes = heads(BACK, EARLY, parts) if late else heads(BACK, 0, EARLY)
        return pltpu.make_async_remote_copy(
            acc.at[1 - side, :, :, lanes], racc.at[:, :, lanes], gpart_s.at[late], gpart_r.at[late],
            device_id={"ctx": partner}, device_id_type=MESH,
        )

    def cell_copy(source, target):
        return pltpu.make_async_remote_copy(
            gbuf, gsub.at[source], ga_s.at[target], ga_r.at[source],
            device_id={"dp": target // 2, "ctx": pair * 2 + target % 2}, device_id_type=MESH,
        )

    def pair_copy(source, target):
        return pltpu.make_async_remote_copy(
            gsub.at[cell], gall.at[source], gb_s.at[target], gb_r.at[source],
            device_id={"ctx": target * 2 + side}, device_id_type=MESH,
        )

    def each(count, body, start=0):
        lax.fori_loop(start, count, lambda i, c: (body(i), c)[1], 0)

    def others(count, me, body):
        each(count, lambda i: pl.when(i != me)(lambda: body(i)))

    def send_rim(i):
        @pl.when(rank < ranks - 1)
        def _():
            for which in range(2):
                rim_copy(i, which).start()

    def send_sums(group):
        each(pairs, lambda t: sum_copy(group, pair, t).start(), pair + 1)

    def collect(some, lanes):
        acc[:, :, :, lanes] = gsum[pl.ds(pair * 2, 2), :, :, lanes].astype(f32)

        def add(s):
            for part in some:
                gsum_copy(part, s, pair).wait_recv()
            acc[:, :, :, lanes] = acc[:, :, :, lanes] + rsum[s, :, :, :, lanes].astype(f32)

        each(pairs, add, pair + 1)

    def load_copy(i, which):
        source, target = ((q_all, q), (do_all, do), (k_all, kx), (v_all, vx))[which]
        rows = pl.ds(BLOCK, length) if which >= 2 else pl.ds(0, length)
        lanes = pl.ds(pl.multiple_of(i * HD, HD), HD)
        return pltpu.make_async_copy(source.at[:, lanes], target.at[i, rows, :], load.at[i, which])

    nb = TILE // BLOCK
    slots = sums.shape[0] * SUMMARY
    before = lax.broadcasted_iota(jnp.int32, (BLOCK, BLOCK), 0) > lax.broadcasted_iota(
        jnp.int32, (BLOCK, BLOCK), 1
    )
    wide = lax.broadcasted_iota(jnp.int32, (BLOCK, TILE), 0) > (
        lax.broadcasted_iota(jnp.int32, (BLOCK, TILE), 1) & (BLOCK - 1)
    )
    there = lax.broadcasted_iota(jnp.int32, (slots, HD), 0) < SUMMARY * rank
    none = jnp.zeros((BLOCK, BLOCK), bf16)

    def cols(h):
        return pl.ds(pl.multiple_of(h * HD, HD), HD)

    def summary(h, which):
        rows = sums[:, which, :, cols(h)].astype(f32).reshape(slots, HD)
        return jnp.where(there, rows, 0.0).astype(bf16)

    def banded(h):
        for i in range(4):
            load_copy(h, i).wait()
        gain = g[:, cols(h)]
        for t in range(length // TILE):
            rows = pl.ds(t * TILE, TILE)
            scaled = (q[h, rows, :].astype(f32) * gain).astype(bf16)
            qs[h, rows, :] = scaled
            skip = 1 if t == 0 else 0
            near = pl.ds((t * nb + skip) * BLOCK, (nb + 1 - skip) * BLOCK)
            for held, ext, other in ((sb, kx, scaled), (db, vx, do[h, rows, :])):
                full = nt(ext[h, near, :], other)
                for i in range(nb):
                    lanes = slice(i * BLOCK, (i + 1) * BLOCK)
                    own = full[(i + 1 - skip) * BLOCK : (i + 2 - skip) * BLOCK, lanes]
                    if i >= skip:
                        own = jnp.where(before, full[(i - skip) * BLOCK : (i + 1 - skip) * BLOCK, lanes], own)
                    held[h % AHEAD, :, pl.ds(t * TILE + i * BLOCK, BLOCK)] = own

    def spread(both):
        strips = []
        for j in range(nb + 1):
            cells = []
            for i in range(nb):
                lanes = slice(i * BLOCK, (i + 1) * BLOCK)
                cells.append(both[j - i][:, lanes] if 0 <= j - i <= 1 else none)
            strips.append(jnp.concatenate(cells, 1))
        return strips

    def softmaxed(h):
        gain = g[:, cols(h)]
        sk, sv = summary(h, 0), summary(h, 1)
        skT, kxT = sk.T, kx[h].T
        dsk = dsv = gp = None
        for t in range(length // TILE):
            rows = pl.ds(t * TILE, TILE)
            near = slice(t * TILE, t * TILE + (nb + 1) * BLOCK)
            scaled, grads = qs[h, rows, :], do[h, rows, :]
            bs, bd = sb[h % AHEAD, :, rows], db[h % AHEAD, :, rows]
            ss, sd = nt(sk, scaled), nt(sv, grads)
            slot = lax.broadcasted_iota(jnp.int32, (slots, TILE), 0)
            if t == 0:
                rs = nt(kx[h, pl.ds(0, BLOCK), :], scaled[:BLOCK])
                rd = nt(vx[h, pl.ds(0, BLOCK), :], grads[:BLOCK])
                rs = jnp.where(rank > 0, rs, NEG)
                bs = jnp.concatenate([jnp.where(before, rs, bs[:, :BLOCK]), bs[:, BLOCK:]], 1)
                bd = jnp.concatenate([jnp.where(before, rd, bd[:, :BLOCK]), bd[:, BLOCK:]], 1)
                spos = slot // SUMMARY * STRIDE + STRIDE - SUMMARY + slot % SUMMARY
                qpos = rank * length + lax.broadcasted_iota(jnp.int32, (slots, TILE), 1)
                seen = qpos - spos >= BLOCK
            else:
                seen = slot < SUMMARY * rank
            ss = jnp.where(seen, ss, NEG)
            top = jnp.maximum(jnp.max(bs, 0, keepdims=True), jnp.max(ss, 0, keepdims=True))
            eb = jnp.exp2((bs - top) * (SCALE * LOG2E))
            es = jnp.exp2((ss - top) * (SCALE * LOG2E))
            inv = 1.0 / (jnp.sum(eb, 0, keepdims=True) + jnp.sum(es, 0, keepdims=True))
            pb, ps = eb * inv, es * inv
            delta = jnp.sum(pb * bd, 0, keepdims=True) + jnp.sum(ps * sd, 0, keepdims=True)
            gb = pb * ((bd - delta) * SCALE)
            gs = (ps * ((sd - delta) * SCALE)).astype(bf16)
            ps = ps.astype(bf16)
            split = lambda x: (jnp.where(wide, x, 0.0).astype(bf16), jnp.where(wide, 0.0, x).astype(bf16))
            pb, gb = split(pb), split(gb)
            for i in range(2):
                pst[h, pl.ds(i * BLOCK, BLOCK), rows] = pb[i]
                gst[h, pl.ds(i * BLOCK, BLOCK), rows] = gb[i]
            pst[h, pl.ds(2 * BLOCK, slots), rows] = ps
            dsv, dsk = plus(dsv, nn(ps, grads)), plus(dsk, nn(gs, scaled))
            if t == 0:
                grim[h, 0] = nn(gb[0][:, :BLOCK], scaled[:BLOCK]).astype(bf16)
                grim[h, 1] = nn(pb[0][:, :BLOCK], grads[:BLOCK]).astype(bf16)
            dq = nn(
                jnp.concatenate([kxT[:, near], skT], 1), jnp.concatenate(spread(gb) + [gs], 0)
            ).T
            gq_ref[rows, cols(h)] = (dq * gain).astype(bf16)
            gp = plus(gp, jnp.sum(dq * q[h, rows, :].astype(f32), 0, keepdims=True))
        for which, x in enumerate((dsk, dsv)):
            gsum[:, which, :, cols(h)] = x.reshape(slots // SUMMARY, SUMMARY, HD).astype(bf16)
        gbuf[pl.ds(h, 1), :] = gp

    def attended(h):
        svT, vxT = summary(h, 1).T, vx[h].T
        dk, dv = [None] * (blocks + 1), [None] * (blocks + 1)
        for t in range(length // TILE):
            rows = pl.ds(t * TILE, TILE)
            near = slice(t * TILE, t * TILE + (nb + 1) * BLOCK)
            first = t * nb
            two = lambda ref: [ref[h, pl.ds(i * BLOCK, BLOCK), rows] for i in range(2)]
            prob = spread(two(pst))
            dscore = spread(two(gst))
            dvt = nn(jnp.concatenate(prob, 0), do[h, rows, :])
            dkt = nn(jnp.concatenate(dscore, 0), qs[h, rows, :])
            for j in range(nb + 1):
                strip = slice(j * BLOCK, (j + 1) * BLOCK)
                dv[first + j] = plus(dv[first + j], dvt[strip])
                dk[first + j] = plus(dk[first + j], dkt[strip])
            full = jnp.concatenate(prob + [pst[h, pl.ds(2 * BLOCK, slots), rows]], 0)
            o_ref[rows, cols(h)] = nn(jnp.concatenate([vxT[:, near], svT], 1), full).T.astype(bf16)
            for n in range(max(first, 1), first + nb):
                gk_ref[pl.ds((n - 1) * BLOCK, BLOCK), cols(h)] = dk[n].astype(bf16)
                gv_ref[pl.ds((n - 1) * BLOCK, BLOCK), cols(h)] = dv[n].astype(bf16)

        @pl.when(rank < ranks - 1)
        def _():
            grim_copy(h).wait_recv()

        later = rank < ranks - 1
        for which, (x, out) in enumerate(((dk[blocks], gk_ref), (dv[blocks], gv_ref))):
            x = x + jnp.where(later, rrim[h, which].astype(f32), 0.0)
            out[pl.ds(last, BLOCK), cols(h)] = x.astype(bf16)
            edge[which, :, cols(h)] = x[BLOCK - 16 :]

    own = [
        pltpu.make_async_copy(full.at[pl.ds(length - SUMMARY, SUMMARY), :], sums.at[rank, i], loc.at[i])
        for i, full in enumerate((k_all, v_all))
    ]
    gains = pltpu.make_async_copy(g_all, g, loc.at[2])
    gains.start()

    def start_load(h):
        for i in range(4):
            load_copy(h, i).start()

    start_load(0)
    for copy in own:
        copy.start()
    each(H, start_load, 1)

    @pl.when(rank == 0)
    def _():
        for i in range(H):
            kx[i, pl.ds(0, BLOCK), :] = jnp.zeros((BLOCK, HD), bf16)
            vx[i, pl.ds(0, BLOCK), :] = jnp.zeros((BLOCK, HD), bf16)

    barrier = pltpu.get_barrier_semaphore()

    def greet(**device):
        pl.semaphore_signal(barrier, inc=1, device_id=device, device_id_type=MESH)

    others(pairs, pair, lambda p: greet(ctx=p * 2 + side))
    others(cells, cell, lambda c: greet(dp=c // 2, ctx=pair * 2 + c % 2))
    beside = rank + 2 * side - 1
    inside = (beside >= 0) & (beside < ranks)

    @pl.when(inside)
    def _():
        greet(ctx=jnp.clip(beside, 0, ranks - 1))

    gains.wait()
    for copy in own:
        copy.wait()
    banded(0)
    pl.semaphore_wait(barrier, pairs - 1 + cells - 1 + inside.astype(jnp.int32))
    part_copy(rank).start()
    each(H, send_rim)

    def early(h):
        @pl.when(h == 2)
        def _():
            part_copy(partner).wait_recv()
            for group in range(groups):
                send_sums(group)

        banded(h)

    each(AHEAD, early, 1)

    def middle(h):
        for group in range(groups):

            @pl.when(h == OUTWARD[group])
            def _(group=group):
                each(pair, lambda s: sum_copy(group, s, pair).wait_recv())

        @pl.when(rank > 0)
        def _():
            for which in range(2):
                rim_copy(h, which).wait_recv()

        @pl.when(h >= AHEAD)
        def _():
            banded(h)

        softmaxed(h)

        @pl.when(rank > 0)
        def _():
            grim_copy(h).start()

        for part in range(parts):

            @pl.when(h == BACK[part + 1] - 1)
            def _(part=part):
                each(pair, lambda t: gsum_copy(part, pair, t).start())

    each(H, middle)
    others(cells, cell, lambda c: cell_copy(cell, c).start())

    def final(h):
        @pl.when(h == 2)
        def _():
            others(cells, cell, lambda c: cell_copy(c, cell).wait_recv())
            gsub[cell] = gbuf[...]
            total = gsub[0]
            for c in range(1, gsub.shape[0]):
                total = total + gsub[c]
            gsub[cell] = total
            gall[pair] = total
            others(pairs, pair, lambda p: pair_copy(pair, p).start())
            collect(range(EARLY), heads(BACK, 0, EARLY))
            gpart_copy(0).start()

        @pl.when(h == 4)
        def _():
            collect(range(EARLY, parts), heads(BACK, EARLY, parts))
            gpart_copy(1).start()

        attended(h)

    each(H, final)

    for group in range(groups):
        each(pairs, lambda t, group=group: sum_copy(group, pair, t).wait_send(), pair + 1)
    part_copy(rank).wait_send()

    @pl.when(rank < ranks - 1)
    def _():
        for i in range(H):
            for which in range(2):
                rim_copy(i, which).wait_send()

    @pl.when(rank > 0)
    def _():
        for i in range(H):
            grim_copy(i).wait_send()

    for part in range(parts):
        each(pair, lambda t, part=part: gsum_copy(part, pair, t).wait_send())
    for late in range(2):
        gpart_copy(late).wait_recv()
    for which, out in enumerate((gk_ref, gv_ref)):
        extra = acc[side, which] + racc[which]
        extra = jnp.concatenate([jnp.zeros((16 - SUMMARY, extra.shape[1]), f32), extra], 0)
        out[pl.ds(length - 16, 16), :] = (edge[which] + extra).astype(bf16)

    others(pairs, pair, lambda p: pair_copy(p, pair).wait_recv())
    total = gall[0]
    for p in range(1, gall.shape[0]):
        total = total + gall[p]
    gain_out[...] = total * (dps * ranks * length) ** -0.5
    others(cells, cell, lambda c: cell_copy(cell, c).wait_send())
    others(pairs, pair, lambda p: pair_copy(pair, p).wait_send())
    for late in range(2):
        gpart_copy(late).wait_send()


def write_kernel(o_in, gq_in, gk_in, gv_in, gain_in, o_out, gq_out, gk_out, gv_out, gain_out, sems):
    length = o_in.shape[0]
    moves = []
    for source, target in ((o_in, o_out), (gq_in, gq_out), (gk_in, gk_out), (gv_in, gv_out)):
        for i in range(2):
            rows = pl.ds(i * (length // 2), length // 2)
            moves.append((source.at[rows], target.at[rows]))
    copies = [pltpu.make_async_copy(a, b, sems.at[i]) for i, (a, b) in enumerate(moves)]
    for copy in copies:
        copy.start()
    for i in range(H):
        gain_out[:, i * HD : (i + 1) * HD] = gain_in[i : i + 1, :]
    for copy in copies:
        copy.wait()


def solution(mesh):
    dps, ranks = mesh.shape["dp"], mesh.shape["ctx"]

    def per_device(queries, keys, values, cotangent, gain):
        _, length, width = queries.shape
        flat = lambda x: x.reshape(length, width)
        q, k, v, do = flat(queries), flat(keys), flat(values), flat(cotangent)
        away = pl.BlockSpec(memory_space=pl.ANY)
        near = pl.BlockSpec(memory_space=pltpu.VMEM)
        far = pl.BlockSpec(memory_space=pltpu.HBM)
        like = jax.ShapeDtypeStruct
        dma = lambda *shape: pltpu.SemaphoreType.DMA(shape)
        groups, parts = len(OUTWARD) - 1, len(BACK) - 1
        slots = ranks * SUMMARY
        held = pl.pallas_call(
            exchange_kernel,
            name="attend_exchange",
            in_specs=[far] * 5,
            out_specs=[near] * 5,
            out_shape=[like((length, width), bf16)] * 4 + [like((H, HD), f32)],
            scratch_shapes=[
                pltpu.VMEM((H, length, HD), bf16),
                pltpu.VMEM((H, length, HD), bf16),
                pltpu.VMEM((H, length, HD), bf16),
                pltpu.VMEM((H, length + BLOCK, HD), bf16),
                pltpu.VMEM((H, length + BLOCK, HD), bf16),
                pltpu.VMEM((1, width), f32),
                pltpu.VMEM((AHEAD, BLOCK, length), f32),
                pltpu.VMEM((AHEAD, BLOCK, length), f32),
                pltpu.VMEM((H, 2 * BLOCK + slots, length), bf16),
                pltpu.VMEM((H, 2 * BLOCK, length), bf16),
                pltpu.VMEM((ranks, 2, SUMMARY, width), bf16),
                pltpu.VMEM((H, 2, BLOCK, HD), bf16),
                pltpu.VMEM((H, 2, BLOCK, HD), bf16),
                pltpu.VMEM((ranks, 2, SUMMARY, width), bf16),
                pltpu.VMEM((ranks // 2, 2, 2, SUMMARY, width), bf16),
                pltpu.VMEM((2, 16, width), f32),
                pltpu.VMEM((2, 2, SUMMARY, width), f32),
                pltpu.VMEM((2, SUMMARY, width), f32),
                pltpu.VMEM((H, HD), f32),
                pltpu.VMEM((dps * 2, H, HD), f32),
                pltpu.VMEM((ranks // 2, H, HD), f32),
                dma(H, 2), dma(H, 2),
                pltpu.SemaphoreType.DMA, pltpu.SemaphoreType.DMA,
                dma(groups, ranks // 2), dma(groups, ranks // 2),
                dma(H), dma(H),
                dma(parts, ranks // 2), dma(parts, ranks // 2),
                dma(2), dma(2),
                dma(dps * 2), dma(dps * 2),
                dma(ranks // 2), dma(ranks // 2),
                dma(3), dma(H, 4),
            ],
            compiler_params=pltpu.CompilerParams(
                collective_id=0, has_side_effects=True, vmem_limit_bytes=44 << 20
            ),
        )(q, do, k, v, gain.reshape(1, width))
        out = pl.pallas_call(
            write_kernel,
            name="attend_write",
            in_specs=[away] * 4 + [near],
            out_specs=[away] * 4 + [near],
            out_shape=[like((length, width), bf16)] * 4 + [like((1, width), f32)],
            scratch_shapes=[dma(8)],
            compiler_params=pltpu.CompilerParams(vmem_limit_bytes=2 << 20),
        )(*held)
        whole = lambda x: x.reshape(1, length, width)
        return whole(out[0]), whole(out[1]), whole(out[2]), whole(out[3]), out[4].reshape(width)

    spread = P("dp", "ctx", None)
    return jax.shard_map(
        per_device,
        mesh=mesh,
        in_specs=(spread,) * 4 + (P(),),
        out_specs=(spread,) * 4 + (P(),),
        check_vma=False,
    )
```

```python
import jax
import jax.numpy as jnp
from jax import lax
from jax.experimental import pallas as pl
from jax.experimental.pallas import tpu as pltpu
from jax.sharding import PartitionSpec as P

f32 = jnp.float32
bf16 = jnp.bfloat16
MESH = pl.DeviceIdType.MESH

H = 8
HD = 128
BLOCK = 128
STRIDE = 1024
SUMMARY = 8
SCALE = HD**-0.5
LOG2E = 1.4426950408889634
NEG = -1e30
TILE = 256
OUTWARD = (0, 1, 2, 4, 6, 8)
OUT_AT = (-1, -1, 0, 2, 4)
BACK = (0, 4, 7, 8)
EARLY = 2
AHEAD = 3
LAG = 4


def nt(a, b):
    return lax.dot_general(a, b, (((1,), (1,)), ((), ())), preferred_element_type=f32)


def nn(a, b):
    return lax.dot_general(a, b, (((1,), (0,)), ((), ())), preferred_element_type=f32)


def plus(old, new):
    return new if old is None else old + new


def exchange_kernel(
    q_all, do_all, k_all, v_all, g_all,
    o_ref, gq_ref, gk_ref, gv_ref, gain_out,
    q, do, qs, kx, vx, g, sb, db, pst, gst, sums, grim, rrim, gsum, rsum, edge, acc, racc, gbuf, gsub, gall,
    rim_s, rim_r, part_s, part_r, sum_s, sum_r, grim_s, grim_r, gsum_s, gsum_r, gpart_s, gpart_r,
    ga_s, ga_r, gb_s, gb_r, loc, load,
):
    dp, rank = lax.axis_index("dp"), lax.axis_index("ctx")
    dps, ranks = lax.axis_size("dp"), lax.axis_size("ctx")
    length = q.shape[1]
    blocks = length // BLOCK
    last = length - BLOCK
    pair, side = rank // 2, rank % 2
    partner = pair * 2 + 1 - side
    cell, cells = dp * 2 + side, dps * 2
    pairs = ranks // 2
    groups, parts = len(OUTWARD) - 1, len(BACK) - 1

    def heads(edges, i, j=None):
        j = i + 1 if j is None else j
        return pl.ds(edges[i] * HD, (edges[j] - edges[i]) * HD)

    def rim_copy(i, which):
        src = (k_all, v_all)[which].at[pl.ds(last, BLOCK), pl.ds(pl.multiple_of(i * HD, HD), HD)]
        return pltpu.make_async_remote_copy(
            src, (kx, vx)[which].at[i, pl.ds(0, BLOCK), :], rim_s.at[i, which], rim_r.at[i, which],
            device_id={"ctx": jnp.minimum(rank + 1, ranks - 1)}, device_id_type=MESH,
        )

    def part_copy(source):
        return pltpu.make_async_remote_copy(
            sums.at[source], sums.at[source], part_s, part_r, device_id={"ctx": partner}, device_id_type=MESH
        )

    def sum_copy(group, source, target):
        both, lanes = pl.ds(source * 2, 2), heads(OUTWARD, group)
        return pltpu.make_async_remote_copy(
            sums.at[both, :, :, lanes], sums.at[both, :, :, lanes], sum_s.at[group, target], sum_r.at[group, source],
            device_id={"ctx": target * 2 + side}, device_id_type=MESH,
        )

    def grim_copy(i):
        return pltpu.make_async_remote_copy(
            grim.at[i], rrim.at[i], grim_s.at[i], grim_r.at[i],
            device_id={"ctx": jnp.maximum(rank - 1, 0)}, device_id_type=MESH,
        )

    def gsum_copy(part, source, target):
        lanes = heads(BACK, part)
        return pltpu.make_async_remote_copy(
            gsum.at[pl.ds(target * 2, 2), :, :, lanes], rsum.at[source, :, :, :, lanes],
            gsum_s.at[part, target], gsum_r.at[part, source],
            device_id={"ctx": target * 2 + side}, device_id_type=MESH,
        )

    def gpart_copy(late):
        lanes = heads(BACK, EARLY, parts) if late else heads(BACK, 0, EARLY)
        return pltpu.make_async_remote_copy(
            acc.at[1 - side, :, :, lanes], racc.at[:, :, lanes], gpart_s.at[late], gpart_r.at[late],
            device_id={"ctx": partner}, device_id_type=MESH,
        )

    def cell_copy(source, target):
        return pltpu.make_async_remote_copy(
            gbuf, gsub.at[source], ga_s.at[target], ga_r.at[source],
            device_id={"dp": target // 2, "ctx": pair * 2 + target % 2}, device_id_type=MESH,
        )

    def pair_copy(source, target):
        return pltpu.make_async_remote_copy(
            gsub.at[cell], gall.at[source], gb_s.at[target], gb_r.at[source],
            device_id={"ctx": target * 2 + side}, device_id_type=MESH,
        )

    def each(count, body, start=0):
        lax.fori_loop(start, count, lambda i, c: (body(i), c)[1], 0)

    def others(count, me, body):
        each(count, lambda i: pl.when(i != me)(lambda: body(i)))

    def send_rim(i):
        @pl.when(rank < ranks - 1)
        def _():
            for which in range(2):
                rim_copy(i, which).start()

    def send_sums(group):
        each(pairs, lambda t: sum_copy(group, pair, t).start(), pair + 1)

    def collect(some, lanes):
        acc[:, :, :, lanes] = gsum[pl.ds(pair * 2, 2), :, :, lanes].astype(f32)

        def add(s):
            for part in some:
                gsum_copy(part, s, pair).wait_recv()
            acc[:, :, :, lanes] = acc[:, :, :, lanes] + rsum[s, :, :, :, lanes].astype(f32)

        each(pairs, add, pair + 1)

    def load_copy(i, which):
        source, target = ((q_all, q), (do_all, do), (k_all, kx), (v_all, vx))[which]
        rows = pl.ds(BLOCK, length) if which >= 2 else pl.ds(0, length)
        lanes = pl.ds(pl.multiple_of(i * HD, HD), HD)
        return pltpu.make_async_copy(source.at[:, lanes], target.at[i, rows, :], load.at[i, which])

    nb = TILE // BLOCK
    slots = sums.shape[0] * SUMMARY
    before = lax.broadcasted_iota(jnp.int32, (BLOCK, BLOCK), 0) > lax.broadcasted_iota(
        jnp.int32, (BLOCK, BLOCK), 1
    )
    wide = lax.broadcasted_iota(jnp.int32, (BLOCK, TILE), 0) > (
        lax.broadcasted_iota(jnp.int32, (BLOCK, TILE), 1) & (BLOCK - 1)
    )
    there = lax.broadcasted_iota(jnp.int32, (slots, HD), 0) < SUMMARY * rank
    none = jnp.zeros((BLOCK, BLOCK), bf16)

    def cols(h):
        return pl.ds(pl.multiple_of(h * HD, HD), HD)

    def summary(h, which):
        rows = sums[:, which, :, cols(h)].astype(f32).reshape(slots, HD)
        return jnp.where(there, rows, 0.0).astype(bf16)

    def banded(h):
        for i in range(4):
            load_copy(h, i).wait()
        gain = g[:, cols(h)]
        for t in range(length // TILE):
            rows = pl.ds(t * TILE, TILE)
            scaled = (q[h, rows, :].astype(f32) * gain).astype(bf16)
            qs[h, rows, :] = scaled
            skip = 1 if t == 0 else 0
            near = pl.ds((t * nb + skip) * BLOCK, (nb + 1 - skip) * BLOCK)
            for held, ext, other in ((sb, kx, scaled), (db, vx, do[h, rows, :])):
                full = nt(ext[h, near, :], other)
                for i in range(nb):
                    lanes = slice(i * BLOCK, (i + 1) * BLOCK)
                    own = full[(i + 1 - skip) * BLOCK : (i + 2 - skip) * BLOCK, lanes]
                    if i >= skip:
                        own = jnp.where(before, full[(i - skip) * BLOCK : (i + 1 - skip) * BLOCK, lanes], own)
                    held[h % AHEAD, :, pl.ds(t * TILE + i * BLOCK, BLOCK)] = own

    def spread(both):
        strips = []
        for j in range(nb + 1):
            cells = []
            for i in range(nb):
                lanes = slice(i * BLOCK, (i + 1) * BLOCK)
                cells.append(both[j - i][:, lanes] if 0 <= j - i <= 1 else none)
            strips.append(jnp.concatenate(cells, 1))
        return strips

    def softmaxed(h):
        gain = g[:, cols(h)]
        sk, sv = summary(h, 0), summary(h, 1)
        skT, kxT = sk.T, kx[h].T
        dsk = dsv = gp = None
        for t in range(length // TILE):
            rows = pl.ds(t * TILE, TILE)
            near = slice(t * TILE, t * TILE + (nb + 1) * BLOCK)
            scaled, grads = qs[h, rows, :], do[h, rows, :]
            bs, bd = sb[h % AHEAD, :, rows], db[h % AHEAD, :, rows]
            ss, sd = nt(sk, scaled), nt(sv, grads)
            slot = lax.broadcasted_iota(jnp.int32, (slots, TILE), 0)
            if t == 0:
                rs = nt(kx[h, pl.ds(0, BLOCK), :], scaled[:BLOCK])
                rd = nt(vx[h, pl.ds(0, BLOCK), :], grads[:BLOCK])
                rs = jnp.where(rank > 0, rs, NEG)
                bs = jnp.concatenate([jnp.where(before, rs, bs[:, :BLOCK]), bs[:, BLOCK:]], 1)
                bd = jnp.concatenate([jnp.where(before, rd, bd[:, :BLOCK]), bd[:, BLOCK:]], 1)
                spos = slot // SUMMARY * STRIDE + STRIDE - SUMMARY + slot % SUMMARY
                qpos = rank * length + lax.broadcasted_iota(jnp.int32, (slots, TILE), 1)
                seen = qpos - spos >= BLOCK
            else:
                seen = slot < SUMMARY * rank
            ss = jnp.where(seen, ss, NEG)
            top = jnp.maximum(jnp.max(bs, 0, keepdims=True), jnp.max(ss, 0, keepdims=True))
            eb = jnp.exp2((bs - top) * (SCALE * LOG2E))
            es = jnp.exp2((ss - top) * (SCALE * LOG2E))
            inv = 1.0 / (jnp.sum(eb, 0, keepdims=True) + jnp.sum(es, 0, keepdims=True))
            pb, ps = eb * inv, es * inv
            delta = jnp.sum(pb * bd, 0, keepdims=True) + jnp.sum(ps * sd, 0, keepdims=True)
            gb = pb * ((bd - delta) * SCALE)
            gs = (ps * ((sd - delta) * SCALE)).astype(bf16)
            ps = ps.astype(bf16)
            split = lambda x: (jnp.where(wide, x, 0.0).astype(bf16), jnp.where(wide, 0.0, x).astype(bf16))
            pb, gb = split(pb), split(gb)
            for i in range(2):
                pst[h, pl.ds(i * BLOCK, BLOCK), rows] = pb[i]
                gst[h, pl.ds(i * BLOCK, BLOCK), rows] = gb[i]
            pst[h, pl.ds(2 * BLOCK, slots), rows] = ps
            dsv, dsk = plus(dsv, nn(ps, grads)), plus(dsk, nn(gs, scaled))
            if t == 0:
                grim[h, 0] = nn(gb[0][:, :BLOCK], scaled[:BLOCK]).astype(bf16)
                grim[h, 1] = nn(pb[0][:, :BLOCK], grads[:BLOCK]).astype(bf16)
            dq = nn(
                jnp.concatenate([kxT[:, near], skT], 1), jnp.concatenate(spread(gb) + [gs], 0)
            ).T
            gq_ref[rows, cols(h)] = (dq * gain).astype(bf16)
            gp = plus(gp, jnp.sum(dq * q[h, rows, :].astype(f32), 0, keepdims=True))
        for which, x in enumerate((dsk, dsv)):
            gsum[:, which, :, cols(h)] = x.reshape(slots // SUMMARY, SUMMARY, HD).astype(bf16)
        gbuf[pl.ds(h, 1), :] = gp

    def attended(h):
        svT, vxT = summary(h, 1).T, vx[h].T
        dk, dv = [None] * (blocks + 1), [None] * (blocks + 1)
        for t in range(length // TILE):
            rows = pl.ds(t * TILE, TILE)
            near = slice(t * TILE, t * TILE + (nb + 1) * BLOCK)
            first = t * nb
            two = lambda ref: [ref[h, pl.ds(i * BLOCK, BLOCK), rows] for i in range(2)]
            prob = spread(two(pst))
            dscore = spread(two(gst))
            dvt = nn(jnp.concatenate(prob, 0), do[h, rows, :])
            dkt = nn(jnp.concatenate(dscore, 0), qs[h, rows, :])
            for j in range(nb + 1):
                strip = slice(j * BLOCK, (j + 1) * BLOCK)
                dv[first + j] = plus(dv[first + j], dvt[strip])
                dk[first + j] = plus(dk[first + j], dkt[strip])
            full = jnp.concatenate(prob + [pst[h, pl.ds(2 * BLOCK, slots), rows]], 0)
            o_ref[rows, cols(h)] = nn(jnp.concatenate([vxT[:, near], svT], 1), full).T.astype(bf16)
            for n in range(max(first, 1), first + nb):
                gk_ref[pl.ds((n - 1) * BLOCK, BLOCK), cols(h)] = dk[n].astype(bf16)
                gv_ref[pl.ds((n - 1) * BLOCK, BLOCK), cols(h)] = dv[n].astype(bf16)

        @pl.when(rank < ranks - 1)
        def _():
            grim_copy(h).wait_recv()

        later = rank < ranks - 1
        for which, (x, out) in enumerate(((dk[blocks], gk_ref), (dv[blocks], gv_ref))):
            x = x + jnp.where(later, rrim[h, which].astype(f32), 0.0)
            out[pl.ds(last, BLOCK), cols(h)] = x.astype(bf16)
            edge[which, :, cols(h)] = x[BLOCK - 16 :]

    own = [
        pltpu.make_async_copy(full.at[pl.ds(length - SUMMARY, SUMMARY), :], sums.at[rank, i], loc.at[i])
        for i, full in enumerate((k_all, v_all))
    ]
    gains = pltpu.make_async_copy(g_all, g, loc.at[2])
    gains.start()

    def start_load(h):
        for i in range(4):
            load_copy(h, i).start()

    start_load(0)
    for copy in own:
        copy.start()
    each(H, start_load, 1)

    @pl.when(rank == 0)
    def _():
        for i in range(H):
            kx[i, pl.ds(0, BLOCK), :] = jnp.zeros((BLOCK, HD), bf16)
            vx[i, pl.ds(0, BLOCK), :] = jnp.zeros((BLOCK, HD), bf16)

    barrier = pltpu.get_barrier_semaphore()

    def greet(**device):
        pl.semaphore_signal(barrier, inc=1, device_id=device, device_id_type=MESH)

    others(pairs, pair, lambda p: greet(ctx=p * 2 + side))
    others(cells, cell, lambda c: greet(dp=c // 2, ctx=pair * 2 + c % 2))
    beside = rank + 2 * side - 1
    inside = (beside >= 0) & (beside < ranks)

    @pl.when(inside)
    def _():
        greet(ctx=jnp.clip(beside, 0, ranks - 1))

    gains.wait()
    for copy in own:
        copy.wait()
    banded(0)
    pl.semaphore_wait(barrier, pairs - 1 + cells - 1 + inside.astype(jnp.int32))
    part_copy(rank).start()
    send_rim(0)
    banded(1)
    part_copy(partner).wait_recv()
    for group in range(groups):
        if OUT_AT[group] < 0:
            send_sums(group)
    send_rim(1)
    each(AHEAD, banded, 2)

    def middle(h):
        @pl.when(h + 2 < H)
        def _():
            send_rim(h + 2)

        for group in range(groups):
            if OUT_AT[group] >= 0:

                @pl.when(h == OUT_AT[group])
                def _(group=group):
                    send_sums(group)

        for group in range(groups):

            @pl.when(h == OUTWARD[group])
            def _(group=group):
                each(pair, lambda s: sum_copy(group, s, pair).wait_recv())

        @pl.when(rank > 0)
        def _():
            for which in range(2):
                rim_copy(h, which).wait_recv()

        softmaxed(h)

        @pl.when(rank > 0)
        def _():
            grim_copy(h).start()

        for part in range(parts):

            @pl.when(h == BACK[part + 1] - 1)
            def _(part=part):
                each(pair, lambda t: gsum_copy(part, pair, t).start())

        @pl.when(h == H - 1)
        def _():
            others(cells, cell, lambda c: cell_copy(cell, c).start())

        @pl.when(h + AHEAD < H)
        def _():
            banded(h + AHEAD)

        @pl.when(h >= LAG)
        def _():
            attended(h - LAG)

    each(H, middle)
    def final(h):
        @pl.when(h == H - LAG + 1)
        def _():
            others(cells, cell, lambda c: cell_copy(c, cell).wait_recv())
            gsub[cell] = gbuf[...]
            total = gsub[0]
            for c in range(1, gsub.shape[0]):
                total = total + gsub[c]
            gsub[cell] = total
            gall[pair] = total
            others(pairs, pair, lambda p: pair_copy(pair, p).start())
            collect(range(EARLY), heads(BACK, 0, EARLY))
            gpart_copy(0).start()

        @pl.when(h == H - LAG + 2)
        def _():
            collect(range(EARLY, parts), heads(BACK, EARLY, parts))
            gpart_copy(1).start()

        attended(h)

    each(H, final, H - LAG)

    for group in range(groups):
        each(pairs, lambda t, group=group: sum_copy(group, pair, t).wait_send(), pair + 1)
    part_copy(rank).wait_send()

    @pl.when(rank < ranks - 1)
    def _():
        for i in range(H):
            for which in range(2):
                rim_copy(i, which).wait_send()

    @pl.when(rank > 0)
    def _():
        for i in range(H):
            grim_copy(i).wait_send()

    for part in range(parts):
        each(pair, lambda t, part=part: gsum_copy(part, pair, t).wait_send())
    for late in range(2):
        gpart_copy(late).wait_recv()
    for which, out in enumerate((gk_ref, gv_ref)):
        extra = acc[side, which] + racc[which]
        extra = jnp.concatenate([jnp.zeros((16 - SUMMARY, extra.shape[1]), f32), extra], 0)
        out[pl.ds(length - 16, 16), :] = (edge[which] + extra).astype(bf16)

    others(pairs, pair, lambda p: pair_copy(p, pair).wait_recv())
    total = gall[0]
    for p in range(1, gall.shape[0]):
        total = total + gall[p]
    gain_out[...] = total * (dps * ranks * length) ** -0.5
    others(cells, cell, lambda c: cell_copy(cell, c).wait_send())
    others(pairs, pair, lambda p: pair_copy(pair, p).wait_send())
    for late in range(2):
        gpart_copy(late).wait_send()


def write_kernel(o_in, gq_in, gk_in, gv_in, gain_in, o_out, gq_out, gk_out, gv_out, gain_out, sems):
    length = o_in.shape[0]
    moves = []
    for source, target in ((o_in, o_out), (gq_in, gq_out), (gk_in, gk_out), (gv_in, gv_out)):
        for i in range(2):
            rows = pl.ds(i * (length // 2), length // 2)
            moves.append((source.at[rows], target.at[rows]))
    copies = [pltpu.make_async_copy(a, b, sems.at[i]) for i, (a, b) in enumerate(moves)]
    for copy in copies:
        copy.start()
    for i in range(H):
        gain_out[:, i * HD : (i + 1) * HD] = gain_in[i : i + 1, :]
    for copy in copies:
        copy.wait()


def solution(mesh):
    dps, ranks = mesh.shape["dp"], mesh.shape["ctx"]

    def per_device(queries, keys, values, cotangent, gain):
        _, length, width = queries.shape
        flat = lambda x: x.reshape(length, width)
        q, k, v, do = flat(queries), flat(keys), flat(values), flat(cotangent)
        away = pl.BlockSpec(memory_space=pl.ANY)
        near = pl.BlockSpec(memory_space=pltpu.VMEM)
        far = pl.BlockSpec(memory_space=pltpu.HBM)
        like = jax.ShapeDtypeStruct
        dma = lambda *shape: pltpu.SemaphoreType.DMA(shape)
        groups, parts = len(OUTWARD) - 1, len(BACK) - 1
        slots = ranks * SUMMARY
        held = pl.pallas_call(
            exchange_kernel,
            name="attend_exchange",
            in_specs=[far] * 5,
            out_specs=[near] * 5,
            out_shape=[like((length, width), bf16)] * 4 + [like((H, HD), f32)],
            scratch_shapes=[
                pltpu.VMEM((H, length, HD), bf16),
                pltpu.VMEM((H, length, HD), bf16),
                pltpu.VMEM((H, length, HD), bf16),
                pltpu.VMEM((H, length + BLOCK, HD), bf16),
                pltpu.VMEM((H, length + BLOCK, HD), bf16),
                pltpu.VMEM((1, width), f32),
                pltpu.VMEM((AHEAD, BLOCK, length), f32),
                pltpu.VMEM((AHEAD, BLOCK, length), f32),
                pltpu.VMEM((H, 2 * BLOCK + slots, length), bf16),
                pltpu.VMEM((H, 2 * BLOCK, length), bf16),
                pltpu.VMEM((ranks, 2, SUMMARY, width), bf16),
                pltpu.VMEM((H, 2, BLOCK, HD), bf16),
                pltpu.VMEM((H, 2, BLOCK, HD), bf16),
                pltpu.VMEM((ranks, 2, SUMMARY, width), bf16),
                pltpu.VMEM((ranks // 2, 2, 2, SUMMARY, width), bf16),
                pltpu.VMEM((2, 16, width), f32),
                pltpu.VMEM((2, 2, SUMMARY, width), f32),
                pltpu.VMEM((2, SUMMARY, width), f32),
                pltpu.VMEM((H, HD), f32),
                pltpu.VMEM((dps * 2, H, HD), f32),
                pltpu.VMEM((ranks // 2, H, HD), f32),
                dma(H, 2), dma(H, 2),
                pltpu.SemaphoreType.DMA, pltpu.SemaphoreType.DMA,
                dma(groups, ranks // 2), dma(groups, ranks // 2),
                dma(H), dma(H),
                dma(parts, ranks // 2), dma(parts, ranks // 2),
                dma(2), dma(2),
                dma(dps * 2), dma(dps * 2),
                dma(ranks // 2), dma(ranks // 2),
                dma(3), dma(H, 4),
            ],
            compiler_params=pltpu.CompilerParams(
                collective_id=0, has_side_effects=True, vmem_limit_bytes=44 << 20
            ),
        )(q, do, k, v, gain.reshape(1, width))
        out = pl.pallas_call(
            write_kernel,
            name="attend_write",
            in_specs=[away] * 4 + [near],
            out_specs=[away] * 4 + [near],
            out_shape=[like((length, width), bf16)] * 4 + [like((1, width), f32)],
            scratch_shapes=[dma(8)],
            compiler_params=pltpu.CompilerParams(vmem_limit_bytes=2 << 20),
        )(*held)
        whole = lambda x: x.reshape(1, length, width)
        return whole(out[0]), whole(out[1]), whole(out[2]), whole(out[3]), out[4].reshape(width)

    spread = P("dp", "ctx", None)
    return jax.shard_map(
        per_device,
        mesh=mesh,
        in_specs=(spread,) * 4 + (P(),),
        out_specs=(spread,) * 4 + (P(),),
        check_vma=False,
    )
```

```python
import jax
import jax.numpy as jnp
from jax import lax
from jax.experimental import pallas as pl
from jax.experimental.pallas import tpu as pltpu
from jax.sharding import PartitionSpec as P

f32 = jnp.float32
bf16 = jnp.bfloat16
MESH = pl.DeviceIdType.MESH

H = 8
HD = 128
BLOCK = 128
STRIDE = 1024
SUMMARY = 8
SCALE = HD**-0.5
LOG2E = 1.4426950408889634
NEG = -1e30
TILE = 256
OUTWARD = (0, 1, 2, 4, 6, 8)
OUT_AT = (-1, -1, 0, 2, 4)
BACK = (0, 4, 7, 8)
EARLY = 2
AHEAD = 3
LAG = 4
LEAD = 3


def nt(a, b):
    return lax.dot_general(a, b, (((1,), (1,)), ((), ())), preferred_element_type=f32)


def nn(a, b):
    return lax.dot_general(a, b, (((1,), (0,)), ((), ())), preferred_element_type=f32)


def plus(old, new):
    return new if old is None else old + new


def exchange_kernel(
    q_all, do_all, k_all, v_all, g_all,
    o_ref, gq_ref, gk_ref, gv_ref, gain_out,
    q, do, qs, kx, vx, g, sb, db, pst, gst, sums, grim, rrim, gsum, rsum, edge, acc, racc, gbuf, gsub, gall,
    rim_s, rim_r, part_s, part_r, sum_s, sum_r, grim_s, grim_r, gsum_s, gsum_r, gpart_s, gpart_r,
    ga_s, ga_r, gb_s, gb_r, loc, load,
):
    dp, rank = lax.axis_index("dp"), lax.axis_index("ctx")
    dps, ranks = lax.axis_size("dp"), lax.axis_size("ctx")
    length = q.shape[1]
    blocks = length // BLOCK
    last = length - BLOCK
    pair, side = rank // 2, rank % 2
    partner = pair * 2 + 1 - side
    cell, cells = dp * 2 + side, dps * 2
    pairs = ranks // 2
    groups, parts = len(OUTWARD) - 1, len(BACK) - 1

    def heads(edges, i, j=None):
        j = i + 1 if j is None else j
        return pl.ds(edges[i] * HD, (edges[j] - edges[i]) * HD)

    def rim_copy(i, which):
        src = (k_all, v_all)[which].at[pl.ds(last, BLOCK), pl.ds(pl.multiple_of(i * HD, HD), HD)]
        return pltpu.make_async_remote_copy(
            src, (kx, vx)[which].at[i, pl.ds(0, BLOCK), :], rim_s.at[i, which], rim_r.at[i, which],
            device_id={"ctx": jnp.minimum(rank + 1, ranks - 1)}, device_id_type=MESH,
        )

    def part_copy(source):
        return pltpu.make_async_remote_copy(
            sums.at[source], sums.at[source], part_s, part_r, device_id={"ctx": partner}, device_id_type=MESH
        )

    def sum_copy(group, source, target):
        both, lanes = pl.ds(source * 2, 2), heads(OUTWARD, group)
        return pltpu.make_async_remote_copy(
            sums.at[both, :, :, lanes], sums.at[both, :, :, lanes], sum_s.at[group, target], sum_r.at[group, source],
            device_id={"ctx": target * 2 + side}, device_id_type=MESH,
        )

    def grim_copy(i):
        return pltpu.make_async_remote_copy(
            grim.at[i], rrim.at[i], grim_s.at[i], grim_r.at[i],
            device_id={"ctx": jnp.maximum(rank - 1, 0)}, device_id_type=MESH,
        )

    def gsum_copy(part, source, target):
        lanes = heads(BACK, part)
        return pltpu.make_async_remote_copy(
            gsum.at[pl.ds(target * 2, 2), :, :, lanes], rsum.at[source, :, :, :, lanes],
            gsum_s.at[part, target], gsum_r.at[part, source],
            device_id={"ctx": target * 2 + side}, device_id_type=MESH,
        )

    def gpart_copy(late):
        lanes = heads(BACK, EARLY, parts) if late else heads(BACK, 0, EARLY)
        return pltpu.make_async_remote_copy(
            acc.at[1 - side, :, :, lanes], racc.at[:, :, lanes], gpart_s.at[late], gpart_r.at[late],
            device_id={"ctx": partner}, device_id_type=MESH,
        )

    def cell_copy(source, target):
        return pltpu.make_async_remote_copy(
            gbuf, gsub.at[source], ga_s.at[target], ga_r.at[source],
            device_id={"dp": target // 2, "ctx": pair * 2 + target % 2}, device_id_type=MESH,
        )

    def pair_copy(source, target):
        return pltpu.make_async_remote_copy(
            gsub.at[cell], gall.at[source], gb_s.at[target], gb_r.at[source],
            device_id={"ctx": target * 2 + side}, device_id_type=MESH,
        )

    def each(count, body, start=0):
        lax.fori_loop(start, count, lambda i, c: (body(i), c)[1], 0)

    def others(count, me, body):
        each(count, lambda i: pl.when(i != me)(lambda: body(i)))

    def send_rim(i):
        @pl.when(rank < ranks - 1)
        def _():
            for which in range(2):
                rim_copy(i, which).start()

    def send_sums(group):
        each(pairs, lambda t: sum_copy(group, pair, t).start(), pair + 1)

    def collect(some, lanes):
        acc[:, :, :, lanes] = gsum[pl.ds(pair * 2, 2), :, :, lanes].astype(f32)

        def add(s):
            for part in some:
                gsum_copy(part, s, pair).wait_recv()
            acc[:, :, :, lanes] = acc[:, :, :, lanes] + rsum[s, :, :, :, lanes].astype(f32)

        each(pairs, add, pair + 1)

    def load_copy(i, which):
        source, target = ((q_all, q), (do_all, do), (k_all, kx), (v_all, vx))[which]
        rows = pl.ds(BLOCK, length) if which >= 2 else pl.ds(0, length)
        lanes = pl.ds(pl.multiple_of(i * HD, HD), HD)
        return pltpu.make_async_copy(source.at[:, lanes], target.at[i, rows, :], load.at[i, which])

    nb = TILE // BLOCK
    slots = sums.shape[0] * SUMMARY
    before = lax.broadcasted_iota(jnp.int32, (BLOCK, BLOCK), 0) > lax.broadcasted_iota(
        jnp.int32, (BLOCK, BLOCK), 1
    )
    wide = lax.broadcasted_iota(jnp.int32, (BLOCK, TILE), 0) > (
        lax.broadcasted_iota(jnp.int32, (BLOCK, TILE), 1) & (BLOCK - 1)
    )
    there = lax.broadcasted_iota(jnp.int32, (slots, HD), 0) < SUMMARY * rank
    none = jnp.zeros((BLOCK, BLOCK), bf16)

    def cols(h):
        return pl.ds(pl.multiple_of(h * HD, HD), HD)

    def summary(h, which):
        rows = sums[:, which, :, cols(h)].astype(f32).reshape(slots, HD)
        return jnp.where(there, rows, 0.0).astype(bf16)

    def banded(h):
        for i in range(4):
            load_copy(h, i).wait()
        gain = g[:, cols(h)]
        for t in range(length // TILE):
            rows = pl.ds(t * TILE, TILE)
            scaled = (q[h, rows, :].astype(f32) * gain).astype(bf16)
            qs[h, rows, :] = scaled
            skip = 1 if t == 0 else 0
            near = pl.ds((t * nb + skip) * BLOCK, (nb + 1 - skip) * BLOCK)
            for held, ext, other in ((sb, kx, scaled), (db, vx, do[h, rows, :])):
                full = nt(ext[h, near, :], other)
                for i in range(nb):
                    lanes = slice(i * BLOCK, (i + 1) * BLOCK)
                    own = full[(i + 1 - skip) * BLOCK : (i + 2 - skip) * BLOCK, lanes]
                    if i >= skip:
                        own = jnp.where(before, full[(i - skip) * BLOCK : (i + 1 - skip) * BLOCK, lanes], own)
                    held[h % AHEAD, :, pl.ds(t * TILE + i * BLOCK, BLOCK)] = own

    def spread(both):
        strips = []
        for j in range(nb + 1):
            cells = []
            for i in range(nb):
                lanes = slice(i * BLOCK, (i + 1) * BLOCK)
                cells.append(both[j - i][:, lanes] if 0 <= j - i <= 1 else none)
            strips.append(jnp.concatenate(cells, 1))
        return strips

    def softmaxed(h):
        gain = g[:, cols(h)]
        sk, sv = summary(h, 0), summary(h, 1)
        skT, kxT = sk.T, kx[h].T
        dsk = dsv = gp = None
        for t in range(length // TILE):
            rows = pl.ds(t * TILE, TILE)
            near = slice(t * TILE, t * TILE + (nb + 1) * BLOCK)
            scaled, grads = qs[h, rows, :], do[h, rows, :]
            bs, bd = sb[h % AHEAD, :, rows], db[h % AHEAD, :, rows]
            ss, sd = nt(sk, scaled), nt(sv, grads)
            slot = lax.broadcasted_iota(jnp.int32, (slots, TILE), 0)
            if t == 0:
                rs = nt(kx[h, pl.ds(0, BLOCK), :], scaled[:BLOCK])
                rd = nt(vx[h, pl.ds(0, BLOCK), :], grads[:BLOCK])
                rs = jnp.where(rank > 0, rs, NEG)
                bs = jnp.concatenate([jnp.where(before, rs, bs[:, :BLOCK]), bs[:, BLOCK:]], 1)
                bd = jnp.concatenate([jnp.where(before, rd, bd[:, :BLOCK]), bd[:, BLOCK:]], 1)
                spos = slot // SUMMARY * STRIDE + STRIDE - SUMMARY + slot % SUMMARY
                qpos = rank * length + lax.broadcasted_iota(jnp.int32, (slots, TILE), 1)
                seen = qpos - spos >= BLOCK
            else:
                seen = slot < SUMMARY * rank
            ss = jnp.where(seen, ss, NEG)
            top = jnp.maximum(jnp.max(bs, 0, keepdims=True), jnp.max(ss, 0, keepdims=True))
            eb = jnp.exp2((bs - top) * (SCALE * LOG2E))
            es = jnp.exp2((ss - top) * (SCALE * LOG2E))
            inv = 1.0 / (jnp.sum(eb, 0, keepdims=True) + jnp.sum(es, 0, keepdims=True))
            pb, ps = eb * inv, es * inv
            delta = jnp.sum(pb * bd, 0, keepdims=True) + jnp.sum(ps * sd, 0, keepdims=True)
            gb = pb * ((bd - delta) * SCALE)
            gs = (ps * ((sd - delta) * SCALE)).astype(bf16)
            ps = ps.astype(bf16)
            split = lambda x: (jnp.where(wide, x, 0.0).astype(bf16), jnp.where(wide, 0.0, x).astype(bf16))
            pb, gb = split(pb), split(gb)
            for i in range(2):
                pst[h, pl.ds(i * BLOCK, BLOCK), rows] = pb[i]
                gst[h, pl.ds(i * BLOCK, BLOCK), rows] = gb[i]
            pst[h, pl.ds(2 * BLOCK, slots), rows] = ps
            dsv, dsk = plus(dsv, nn(ps, grads)), plus(dsk, nn(gs, scaled))
            if t == 0:
                grim[h, 0] = nn(gb[0][:, :BLOCK], scaled[:BLOCK]).astype(bf16)
                grim[h, 1] = nn(pb[0][:, :BLOCK], grads[:BLOCK]).astype(bf16)
            dq = nn(
                jnp.concatenate([kxT[:, near], skT], 1), jnp.concatenate(spread(gb) + [gs], 0)
            ).T
            gq_ref[rows, cols(h)] = (dq * gain).astype(bf16)
            gp = plus(gp, jnp.sum(dq * q[h, rows, :].astype(f32), 0, keepdims=True))
        for which, x in enumerate((dsk, dsv)):
            gsum[:, which, :, cols(h)] = x.reshape(slots // SUMMARY, SUMMARY, HD).astype(bf16)
        gbuf[pl.ds(h, 1), :] = gp

    def attended(h):
        svT, vxT = summary(h, 1).T, vx[h].T
        dk, dv = [None] * (blocks + 1), [None] * (blocks + 1)
        for t in range(length // TILE):
            rows = pl.ds(t * TILE, TILE)
            near = slice(t * TILE, t * TILE + (nb + 1) * BLOCK)
            first = t * nb
            two = lambda ref: [ref[h, pl.ds(i * BLOCK, BLOCK), rows] for i in range(2)]
            prob = spread(two(pst))
            dscore = spread(two(gst))
            dvt = nn(jnp.concatenate(prob, 0), do[h, rows, :])
            dkt = nn(jnp.concatenate(dscore, 0), qs[h, rows, :])
            for j in range(nb + 1):
                strip = slice(j * BLOCK, (j + 1) * BLOCK)
                dv[first + j] = plus(dv[first + j], dvt[strip])
                dk[first + j] = plus(dk[first + j], dkt[strip])
            full = jnp.concatenate(prob + [pst[h, pl.ds(2 * BLOCK, slots), rows]], 0)
            o_ref[rows, cols(h)] = nn(jnp.concatenate([vxT[:, near], svT], 1), full).T.astype(bf16)
            for n in range(max(first, 1), first + nb):
                gk_ref[pl.ds((n - 1) * BLOCK, BLOCK), cols(h)] = dk[n].astype(bf16)
                gv_ref[pl.ds((n - 1) * BLOCK, BLOCK), cols(h)] = dv[n].astype(bf16)

        @pl.when(rank < ranks - 1)
        def _():
            grim_copy(h).wait_recv()

        later = rank < ranks - 1
        for which, (x, out) in enumerate(((dk[blocks], gk_ref), (dv[blocks], gv_ref))):
            x = x + jnp.where(later, rrim[h, which].astype(f32), 0.0)
            out[pl.ds(last, BLOCK), cols(h)] = x.astype(bf16)
            edge[which, :, cols(h)] = x[BLOCK - 16 :]

    own = [
        pltpu.make_async_copy(full.at[pl.ds(length - SUMMARY, SUMMARY), :], sums.at[rank, i], loc.at[i])
        for i, full in enumerate((k_all, v_all))
    ]
    gains = pltpu.make_async_copy(g_all, g, loc.at[2])
    gains.start()

    def start_load(h):
        for i in range(4):
            load_copy(h, i).start()

    start_load(0)
    for copy in own:
        copy.start()
    each(H, start_load, 1)

    @pl.when(rank == 0)
    def _():
        for i in range(H):
            kx[i, pl.ds(0, BLOCK), :] = jnp.zeros((BLOCK, HD), bf16)
            vx[i, pl.ds(0, BLOCK), :] = jnp.zeros((BLOCK, HD), bf16)

    barrier = pltpu.get_barrier_semaphore()

    def greet(**device):
        pl.semaphore_signal(barrier, inc=1, device_id=device, device_id_type=MESH)

    others(pairs, pair, lambda p: greet(ctx=p * 2 + side))
    others(cells, cell, lambda c: greet(dp=c // 2, ctx=pair * 2 + c % 2))
    beside = rank + 2 * side - 1
    inside = (beside >= 0) & (beside < ranks)

    @pl.when(inside)
    def _():
        greet(ctx=jnp.clip(beside, 0, ranks - 1))

    gains.wait()
    for copy in own:
        copy.wait()
    banded(0)
    pl.semaphore_wait(barrier, pairs - 1 + cells - 1 + inside.astype(jnp.int32))
    part_copy(rank).start()
    send_rim(0)
    send_rim(1)
    banded(1)
    part_copy(partner).wait_recv()
    for group in range(groups):
        if OUT_AT[group] < 0:
            send_sums(group)
    for i in range(2, LEAD):
        send_rim(i)
    each(AHEAD, banded, 2)

    def middle(h):
        @pl.when(h + LEAD < H)
        def _():
            send_rim(h + LEAD)

        for group in range(groups):
            if OUT_AT[group] >= 0:

                @pl.when(h == OUT_AT[group])
                def _(group=group):
                    send_sums(group)

        for group in range(groups):

            @pl.when(h == OUTWARD[group])
            def _(group=group):
                each(pair, lambda s: sum_copy(group, s, pair).wait_recv())

        @pl.when(rank > 0)
        def _():
            for which in range(2):
                rim_copy(h, which).wait_recv()

        softmaxed(h)

        @pl.when(rank > 0)
        def _():
            grim_copy(h).start()

        for part in range(parts):

            @pl.when(h == BACK[part + 1] - 1)
            def _(part=part):
                each(pair, lambda t: gsum_copy(part, pair, t).start())

        @pl.when(h == H - 1)
        def _():
            others(cells, cell, lambda c: cell_copy(cell, c).start())

        @pl.when(h + AHEAD < H)
        def _():
            banded(h + AHEAD)

        @pl.when(h >= LAG)
        def _():
            attended(h - LAG)

    each(H, middle)
    def final(h):
        @pl.when(h == H - LAG + 1)
        def _():
            others(cells, cell, lambda c: cell_copy(c, cell).wait_recv())
            gsub[cell] = gbuf[...]
            total = gsub[0]
            for c in range(1, gsub.shape[0]):
                total = total + gsub[c]
            gsub[cell] = total
            gall[pair] = total
            others(pairs, pair, lambda p: pair_copy(pair, p).start())
            collect(range(EARLY), heads(BACK, 0, EARLY))
            gpart_copy(0).start()

        @pl.when(h == H - LAG + 2)
        def _():
            collect(range(EARLY, parts), heads(BACK, EARLY, parts))
            gpart_copy(1).start()

        attended(h)

    each(H, final, H - LAG)

    for group in range(groups):
        each(pairs, lambda t, group=group: sum_copy(group, pair, t).wait_send(), pair + 1)
    part_copy(rank).wait_send()

    @pl.when(rank < ranks - 1)
    def _():
        for i in range(H):
            for which in range(2):
                rim_copy(i, which).wait_send()

    @pl.when(rank > 0)
    def _():
        for i in range(H):
            grim_copy(i).wait_send()

    for part in range(parts):
        each(pair, lambda t, part=part: gsum_copy(part, pair, t).wait_send())
    for late in range(2):
        gpart_copy(late).wait_recv()
    for which, out in enumerate((gk_ref, gv_ref)):
        extra = acc[side, which] + racc[which]
        extra = jnp.concatenate([jnp.zeros((16 - SUMMARY, extra.shape[1]), f32), extra], 0)
        out[pl.ds(length - 16, 16), :] = (edge[which] + extra).astype(bf16)

    others(pairs, pair, lambda p: pair_copy(p, pair).wait_recv())
    total = gall[0]
    for p in range(1, gall.shape[0]):
        total = total + gall[p]
    gain_out[...] = total * (dps * ranks * length) ** -0.5
    others(cells, cell, lambda c: cell_copy(cell, c).wait_send())
    others(pairs, pair, lambda p: pair_copy(pair, p).wait_send())
    for late in range(2):
        gpart_copy(late).wait_send()


def write_kernel(o_in, gq_in, gk_in, gv_in, gain_in, o_out, gq_out, gk_out, gv_out, gain_out, sems):
    length = o_in.shape[0]
    moves = []
    for source, target in ((o_in, o_out), (gq_in, gq_out), (gk_in, gk_out), (gv_in, gv_out)):
        for i in range(2):
            rows = pl.ds(i * (length // 2), length // 2)
            moves.append((source.at[rows], target.at[rows]))
    copies = [pltpu.make_async_copy(a, b, sems.at[i]) for i, (a, b) in enumerate(moves)]
    for copy in copies:
        copy.start()
    for i in range(H):
        gain_out[:, i * HD : (i + 1) * HD] = gain_in[i : i + 1, :]
    for copy in copies:
        copy.wait()


def solution(mesh):
    dps, ranks = mesh.shape["dp"], mesh.shape["ctx"]

    def per_device(queries, keys, values, cotangent, gain):
        _, length, width = queries.shape
        flat = lambda x: x.reshape(length, width)
        q, k, v, do = flat(queries), flat(keys), flat(values), flat(cotangent)
        away = pl.BlockSpec(memory_space=pl.ANY)
        near = pl.BlockSpec(memory_space=pltpu.VMEM)
        far = pl.BlockSpec(memory_space=pltpu.HBM)
        like = jax.ShapeDtypeStruct
        dma = lambda *shape: pltpu.SemaphoreType.DMA(shape)
        groups, parts = len(OUTWARD) - 1, len(BACK) - 1
        slots = ranks * SUMMARY
        held = pl.pallas_call(
            exchange_kernel,
            name="attend_exchange",
            in_specs=[far] * 5,
            out_specs=[near] * 5,
            out_shape=[like((length, width), bf16)] * 4 + [like((H, HD), f32)],
            scratch_shapes=[
                pltpu.VMEM((H, length, HD), bf16),
                pltpu.VMEM((H, length, HD), bf16),
                pltpu.VMEM((H, length, HD), bf16),
                pltpu.VMEM((H, length + BLOCK, HD), bf16),
                pltpu.VMEM((H, length + BLOCK, HD), bf16),
                pltpu.VMEM((1, width), f32),
                pltpu.VMEM((AHEAD, BLOCK, length), f32),
                pltpu.VMEM((AHEAD, BLOCK, length), f32),
                pltpu.VMEM((H, 2 * BLOCK + slots, length), bf16),
                pltpu.VMEM((H, 2 * BLOCK, length), bf16),
                pltpu.VMEM((ranks, 2, SUMMARY, width), bf16),
                pltpu.VMEM((H, 2, BLOCK, HD), bf16),
                pltpu.VMEM((H, 2, BLOCK, HD), bf16),
                pltpu.VMEM((ranks, 2, SUMMARY, width), bf16),
                pltpu.VMEM((ranks // 2, 2, 2, SUMMARY, width), bf16),
                pltpu.VMEM((2, 16, width), f32),
                pltpu.VMEM((2, 2, SUMMARY, width), f32),
                pltpu.VMEM((2, SUMMARY, width), f32),
                pltpu.VMEM((H, HD), f32),
                pltpu.VMEM((dps * 2, H, HD), f32),
                pltpu.VMEM((ranks // 2, H, HD), f32),
                dma(H, 2), dma(H, 2),
                pltpu.SemaphoreType.DMA, pltpu.SemaphoreType.DMA,
                dma(groups, ranks // 2), dma(groups, ranks // 2),
                dma(H), dma(H),
                dma(parts, ranks // 2), dma(parts, ranks // 2),
                dma(2), dma(2),
                dma(dps * 2), dma(dps * 2),
                dma(ranks // 2), dma(ranks // 2),
                dma(3), dma(H, 4),
            ],
            compiler_params=pltpu.CompilerParams(
                collective_id=0, has_side_effects=True, vmem_limit_bytes=44 << 20
            ),
        )(q, do, k, v, gain.reshape(1, width))
        out = pl.pallas_call(
            write_kernel,
            name="attend_write",
            in_specs=[away] * 4 + [near],
            out_specs=[away] * 4 + [near],
            out_shape=[like((length, width), bf16)] * 4 + [like((1, width), f32)],
            scratch_shapes=[dma(8)],
            compiler_params=pltpu.CompilerParams(vmem_limit_bytes=2 << 20),
        )(*held)
        whole = lambda x: x.reshape(1, length, width)
        return whole(out[0]), whole(out[1]), whole(out[2]), whole(out[3]), out[4].reshape(width)

    spread = P("dp", "ctx", None)
    return jax.shard_map(
        per_device,
        mesh=mesh,
        in_specs=(spread,) * 4 + (P(),),
        out_specs=(spread,) * 4 + (P(),),
        check_vma=False,
    )
```
